256 devices in a mesh: rows: 64 (over z, y, core), rep: 4 (over x).
Axes of the slice: x: 4, y: 4, z: 8, core: 2. Of those that a mesh axis runs over, the one named last changes fastest.
Arguments:
- features: bfloat16 [262144, 256], P(('rows', 'rep')), may hold values from -6 to 6
- weight: bfloat16 [256, 256], replicated, may hold values from -0.375 to 0.375
- block_cols: int32 [2048, 4, 2], P('rows', 'rep'), may hold values from 0 to 511, as said below
- block_vals: bfloat16 [2048, 4, 2, 128, 128], P('rows', 'rep'), as said below
- out_grad: bfloat16 [262144, 256], P('rows'), may hold values from -6 to 6
Outputs:
- activations: bfloat16 [262144, 256], P(('rows', 'rep'))
- input_grad: bfloat16 [262144, 256], P(('rows', 'rep'))
- weight_grad: float32 [256, 256], replicated
The draws below stay inside these ranges and needn't reach their ends.
Inputs may be any that keep to these rules, and one draw needn't show every extreme that they name: `block_cols`: layer c's k-th block column is global block column (k // 8) * 32 + c * 8 + k % 8, whose rows the device of index k // 8 along rows holds in layer c. In the layer that owns a block row, slot 0 is its diagonal block; no other held block of a device lies in its own block columns. For every layer, every device along rows and every other device along rows, at most 1 of the first device's held blocks in that layer lie in block columns of the other, and in every draw some pair has exactly 1. `block_vals`: the adjacency is symmetric: every held block at block row b, block column g in slot s has a partner held at block row g, block column b in slot s (of the layer owning b) that is its transpose; diagonal blocks are symmetric.
All inputs are finite; a program needn't handle non-finite values.
Results may differ from the reference program's by a relative error of at most 0.006.
Values may be sent and summed in bfloat16 or wider, within the bound.
A program may use at most 128 MiB of HBM per device.

```python
import math
import jax
import jax.numpy as jnp
from jax import lax

WIDTH = 256
BLOCK = 128
SLOTS = 2
ROW_BLOCKS = 32
OWN_BLOCKS = 8
BLOCKS = 2048
NODES = 262144
N_ROWS = 64
N_REP = 4


def block_layout(base_key):
    group_count = N_ROWS
    class_count = N_ROWS // 2 - 1
    couple_count = SLOTS * OWN_BLOCKS // 2
    rotation_order = jax.random.permutation(jax.random.fold_in(base_key, 71), group_count).astype(jnp.int32)
    rotation_place = jnp.zeros_like(rotation_order).at[rotation_order].set(jnp.arange(group_count, dtype=jnp.int32))
    shuffle = jax.random.permutation(jax.random.fold_in(base_key, 72), class_count).astype(jnp.int32)
    full_shape = (BLOCKS, N_REP, SLOTS)
    blocks = jnp.arange(BLOCKS, dtype=jnp.int32)[:, None, None]
    home_group = jnp.broadcast_to(blocks // ROW_BLOCKS, full_shape)
    home_class = jnp.broadcast_to(blocks % ROW_BLOCKS // OWN_BLOCKS, full_shape)
    home_place = jnp.broadcast_to(blocks % OWN_BLOCKS, full_shape)
    layer_ids = jnp.broadcast_to(jnp.arange(N_REP, dtype=jnp.int32)[None, :, None], full_shape)
    slot_index = jnp.broadcast_to(jnp.arange(SLOTS, dtype=jnp.int32)[None, None, :], full_shape)
    own_layer = layer_ids == home_class
    item_index = slot_index * OWN_BLOCKS + home_place
    pair_running = (jnp.bitwise_xor(home_class, layer_ids) - 1) * couple_count + item_index // 2
    own_running = (N_REP - 1) * couple_count + home_place // 2
    running = jnp.where(own_layer, own_running, pair_running)
    offset_size = 1 + shuffle[running % class_count]
    parity = jnp.where(jnp.where(own_layer, home_place, item_index) % 2 == 0, 1, -1)
    direction = jnp.where(layer_ids > home_class, 1, -1)
    offset_step = jnp.where(own_layer, parity, parity * direction) * offset_size
    target_group = rotation_order[(rotation_place[home_group] + offset_step) % group_count]
    target_place = jnp.where(own_layer, jnp.bitwise_xor(home_place, 1), home_place)
    diagonal = own_layer & (slot_index == 0)
    target_group = jnp.where(diagonal, home_group, target_group)
    target_place = jnp.where(diagonal, home_place, target_place)
    columns = (target_group * OWN_BLOCKS + target_place).astype(jnp.int32)
    partner_row = target_group * ROW_BLOCKS + layer_ids * OWN_BLOCKS + target_place
    partner_flat = (partner_row * N_REP + home_class) * SLOTS + slot_index
    leading = (layer_ids > home_class) | own_layer & (slot_index > 0) & (home_place % 2 == 0)
    return (columns, partner_flat, leading, diagonal)


def draw_block_cols(key, part):
    return block_layout(key)[0]


def draw_block_vals(key, part):
    columns, partner_flat, leading, diagonal = block_layout(key)
    value_scale = (SLOTS * N_REP * BLOCK) ** (-0.5)
    self_flat = jnp.arange(BLOCKS * N_REP * SLOTS, dtype=jnp.int32).reshape(BLOCKS, N_REP, SLOTS)
    source_flat = jnp.where(leading | diagonal, self_flat, partner_flat).reshape(-1)
    value_key = jax.random.fold_in(key, 73)
    drawn = jax.vmap(lambda index: jax.random.normal(jax.random.fold_in(value_key, index), (BLOCK, BLOCK), jnp.float32))(source_flat)
    drawn = drawn.reshape(BLOCKS, N_REP, SLOTS, BLOCK, BLOCK) * value_scale
    turned = jnp.swapaxes(drawn, -1, -2)
    symmetric = (drawn + turned) * math.sqrt(0.5)
    result = jnp.where(diagonal[..., None, None], symmetric, jnp.where(leading[..., None, None], drawn, turned))
    return result.astype(jnp.bfloat16)


def level_of(own_key, shape, shards, low, top_value):
    loudness = 1.0
    for position, shards_of in shards:
        steps = jax.random.uniform(jax.random.fold_in(jax.random.fold_in(own_key, 6), position), (shards_of,), jnp.float32, low / len(shards), top_value / len(shards))
        loudness = loudness * jnp.repeat(jnp.exp(steps), shape[position] // shards_of).reshape((-1,) + (1,) * (len(shape) - 1 - position))
    return loudness


def gaussian(key, shape, scale, limit, split=(), kind=jnp.bfloat16):
    gain = level_of(key, shape, split, -0.22, 0.18) if split else 1.0
    entries = jax.random.normal(key, shape, jnp.float32) * scale * gain
    return jnp.minimum(jnp.maximum(entries, -limit), limit).astype(kind)


def setup_inputs(seed: int = 0) -> dict:
    key_list = jax.random.split(jax.random.key(seed), 6)
    return {
        "features": gaussian(key_list[0], (NODES, WIDTH), 1.0, 6.0, ((0, 256),)),
        "weight": gaussian(key_list[1], (WIDTH, WIDTH), WIDTH ** -0.5, 0.375),
        "block_cols": draw_block_cols(jax.random.fold_in(key_list[5], 71), 0),
        "block_vals": draw_block_vals(jax.random.fold_in(key_list[5], 71), 0),
        "out_grad": gaussian(key_list[4], (NODES, WIDTH), 1.0, 6.0, ((0, 64),)),
    }


def silu_parts(summed):
    sigmoid_vals = jax.nn.sigmoid(summed)
    return (summed * sigmoid_vals, sigmoid_vals * (1.0 + summed * (1.0 - sigmoid_vals)))

def column_blocks(block_cols):
    layer_ids = jnp.arange(N_REP, dtype=jnp.int32)[None, :, None]
    return block_cols // OWN_BLOCKS * ROW_BLOCKS + layer_ids * OWN_BLOCKS + block_cols % OWN_BLOCKS

def reference(features, weight, block_cols, block_vals, out_grad):
    mixed_rows = jnp.dot(features, weight, preferred_element_type=jnp.float32).astype(jnp.bfloat16)
    targets = column_blocks(block_cols)
    mixed_blocks = mixed_rows.reshape(BLOCKS, BLOCK, WIDTH)
    layer_range = jnp.arange(N_REP, dtype=jnp.int32)

    def forward_layer(running, layer_index):
        layer_vals = block_vals[:, layer_index].astype(jnp.float32)
        fetched = jnp.take(mixed_blocks, targets[:, layer_index], axis=0).astype(jnp.float32)
        return (running + jnp.einsum('bsij,bsjf->bif', layer_vals, fetched, precision=lax.Precision.HIGHEST), None)
    summed, _ = lax.scan(forward_layer, jnp.zeros((BLOCKS, BLOCK, WIDTH), jnp.float32), layer_range)
    summed = summed.reshape(NODES, WIDTH)
    values_all, slopes_all = silu_parts(summed)
    activations = values_all.astype(jnp.bfloat16)
    masked = (out_grad.astype(jnp.float32) * slopes_all).astype(jnp.bfloat16)
    grad_blocks = masked.reshape(BLOCKS, BLOCK, WIDTH).astype(jnp.float32)

    def backward_layer(running, layer_index):
        layer_vals = block_vals[:, layer_index].astype(jnp.float32)
        slot_terms = jnp.einsum('bsji,bjf->bsif', layer_vals, grad_blocks, precision=lax.Precision.HIGHEST)
        spread = jax.ops.segment_sum(slot_terms.reshape(BLOCKS * SLOTS, BLOCK, WIDTH), targets[:, layer_index].reshape(-1), num_segments=BLOCKS)
        return (running + spread, None)
    back_rows, _ = lax.scan(backward_layer, jnp.zeros((BLOCKS, BLOCK, WIDTH), jnp.float32), layer_range)
    back_rows = back_rows.reshape(NODES, WIDTH)
    weight_grad = jnp.dot(features.astype(jnp.float32).T, back_rows, precision=lax.Precision.HIGHEST) * (1.0 / math.sqrt(NODES))
    input_grad = jnp.dot(back_rows.astype(jnp.bfloat16), weight.T, preferred_element_type=jnp.float32).astype(jnp.bfloat16)
    return (activations, input_grad, weight_grad)
```

```python
import functools
import math

import jax
import jax.numpy as jnp
from jax import lax
from jax.experimental import pallas as pl
from jax.experimental.pallas import tpu as pltpu
from jax.sharding import PartitionSpec as P

MESH = pl.DeviceIdType.MESH
Z = 8
YC = 8
X = 4
B = 128
LANES = 128
OWN = 8
F32 = jnp.float32
BF16 = jnp.bfloat16


def place():
    r, c = lax.axis_index("rows"), lax.axis_index("rep")
    return r, r // YC, r % YC, c


def greet(partners):
    barrier = pltpu.get_barrier_semaphore()
    for device in partners:
        pl.semaphore_signal(barrier, inc=1, device_id=device, device_id_type=MESH)
    pl.semaphore_wait(barrier, len(partners))


def remote(src, dst, send, recv, device):
    return pltpu.make_async_remote_copy(
        src_ref=src, dst_ref=dst, send_sem=send, recv_sem=recv, device_id=device, device_id_type=MESH
    )


def wait_bytes(ref, sem):
    pltpu.make_async_copy(ref, ref, sem).wait()


def table_kernel(own_ref, out_ref, got, send, recv):
    r, z, yc, c = place()
    greet([(z * YC + (yc + 1 + j) % YC, c) for j in range(YC - 1)])
    copies = [
        remote(own_ref, got.at[j], send.at[j], recv.at[j], (z * YC + (yc + 1 + j) % YC, c)) for j in range(YC - 1)
    ]
    for copy in copies:
        copy.start()
    for copy in copies:
        copy.wait()
    out_ref[0 : YC - 1] = got[...]
    out_ref[YC - 1] = own_ref[...]


def exchange_tables(own):
    return pl.pallas_call(
        table_kernel,
        out_shape=jax.ShapeDtypeStruct((YC, 8, LANES), jnp.int32),
        in_specs=[pl.BlockSpec(memory_space=pltpu.VMEM)],
        out_specs=pl.BlockSpec(memory_space=pltpu.VMEM),
        scratch_shapes=[
            pltpu.VMEM((YC - 1, 8, LANES), jnp.int32),
            pltpu.SemaphoreType.DMA((YC - 1,)),
            pltpu.SemaphoreType.DMA((YC - 1,)),
        ],
        compiler_params=pltpu.CompilerParams(collective_id=0, has_side_effects=True),
    )(own)


def spmm_kernel(tab, idx, x_ref, vals_ref, out_ref, *scratch):
    ag = [scratch[h * Z : (h + 1) * Z] for h in range(2)]
    sbuf, src, xs, xr, own = (scratch[16 + 2 * i : 18 + 2 * i] for i in range(5))
    z_send, z_recv, y_send, y_recv, x_send, x_recv = scratch[26:]
    r, z, yc, c = place()
    up, down = (z + 1) % Z * YC + yc, (z + Z - 1) % Z * YC + yc
    greet(
        [(up, c), (down, c)]
        + [(z * YC + (yc + 1 + j) % YC, c) for j in range(YC - 1)]
        + [(r, (c + d) % X) for d in range(1, X)]
    )
    half = OWN // 2

    def hop(h, k, forward):
        source = x_ref.at[:, :, pl.ds(h * LANES, LANES)] if k == 0 else ag[h][k]
        nxt = (k + 1) % Z if forward else (k - 1) % Z
        target = ag[h][nxt]
        lane = 0 if forward else 1
        if nxt == Z // 2:
            rows = pl.ds(0, half) if forward else pl.ds(half, half)
            source, target = source.at[rows], target.at[rows]
        return remote(
            source, target, z_send.at[h, nxt, lane], z_recv.at[h, nxt, lane], (up if forward else down, c)
        )

    def arrived(h, k, lane):
        if k == Z // 2:
            part = ag[h][k].at[pl.ds(0 if lane == 0 else half, half)]
        else:
            part = ag[h][k]
        wait_bytes(part, z_recv.at[h, k, lane])

    def load_block(h, k, p):
        if k == 0:
            return x_ref[p, :, pl.ds(h * LANES, LANES)]
        return ag[h][k][p]

    def serve(h, k):
        column = (z - k + Z) % Z * YC + yc

        def pick(j, _):
            sbuf[h][j * Z + k] = load_block(h, k, tab[YC - 2 - j, column])
            return 0

        lax.fori_loop(0, YC - 1, pick, 0)
        if k == 0:
            for p in range(OWN):
                src[h][YC * Z + p] = x_ref[p, :, pl.ds(h * LANES, LANES)]
        else:
            src[h][(YC - 1) * Z + k] = load_block(h, k, tab[YC - 1, column])

        def post(j, _):
            remote(
                sbuf[h].at[j * Z + k],
                src[h].at[j * Z + k],
                y_send.at[h],
                y_recv.at[h],
                (z * YC + (yc + 1 + j) % YC, c),
            ).start()
            return 0

        lax.fori_loop(0, YC - 1, post, 0)

    def products(h, d):
        first = (c + d) % X * OWN

        def row(p, _):
            b = first + p
            total = jnp.dot(vals_ref[b, 0], src[h][idx[2 * b]], preferred_element_type=F32)
            total += jnp.dot(vals_ref[b, 1], src[h][idx[2 * b + 1]], preferred_element_type=F32)
            if d == 0:
                own[h][p] = total
            else:
                xs[h][(d - 1) * OWN + p] = total
                slot = (d - 1) * OWN + p
                remote(
                    xs[h].at[slot], xr[h].at[slot], x_send.at[h], x_recv.at[h], (r, (c + d) % X)
                ).start()
            return 0

        lax.fori_loop(0, OWN, row, 0)

    def collect(h):
        wait_bytes(xr[h], x_recv.at[h])

        def row(p, _):
            out_ref[p, :, pl.ds(h * LANES, LANES)] = (own[h][p] + xr[h][p]) + (xr[h][OWN + p] + xr[h][2 * OWN + p])
            return 0

        lax.fori_loop(0, OWN, row, 0)

    def ring(h, step):
        if step < Z // 2:
            arrived(h, step, 0)
            hop(h, step, True).start()
            arrived(h, Z - step, 1)
            hop(h, Z - step, False).start()
            serve(h, step)
            serve(h, Z - step)
        else:
            arrived(h, step, 0)
            arrived(h, step, 1)
            serve(h, step)

    def begin(h):
        hop(h, 0, True).start()
        hop(h, 0, False).start()

    begin(0)
    serve(0, 0)
    ring(0, 1)
    begin(1)
    serve(1, 0)
    ring(0, 2)
    ring(1, 1)
    ring(0, 3)
    ring(1, 2)
    ring(0, 4)
    wait_bytes(src[0].at[pl.ds(0, (YC - 1) * Z)], y_recv.at[0])
    products(0, 2)
    ring(1, 3)
    products(0, 1)
    products(0, 3)
    products(0, 0)
    ring(1, 4)
    wait_bytes(src[1].at[pl.ds(0, (YC - 1) * Z)], y_recv.at[1])
    for d in (2, 1, 3, 0):
        products(1, d)
    collect(0)
    collect(1)
    for h in range(2):
        for k in range(Z // 2):
            hop(h, k, True).wait_send()
            hop(h, (Z - k) % Z, False).wait_send()
        wait_bytes(sbuf[h], y_send.at[h])
        wait_bytes(xs[h], x_send.at[h])


def spmm(tab, idx, x, vals):
    blocks = lambda n, kind: pltpu.VMEM((n, B, LANES), kind)
    smem = pl.BlockSpec(memory_space=pltpu.SMEM)
    vmem = pl.BlockSpec(memory_space=pltpu.VMEM)
    return pl.pallas_call(
        spmm_kernel,
        out_shape=jax.ShapeDtypeStruct((OWN, B, 2 * LANES), F32),
        in_specs=[smem, smem, vmem, vmem],
        out_specs=vmem,
        scratch_shapes=[blocks(OWN, BF16) for _ in range(2 * Z)]
        + [blocks((YC - 1) * Z, BF16)] * 2
        + [blocks(YC * Z + OWN, BF16)] * 2
        + [blocks((X - 1) * OWN, F32)] * 2
        + [blocks((X - 1) * OWN, F32)] * 2
        + [blocks(OWN, F32)] * 2
        + [
            pltpu.SemaphoreType.DMA((2, Z, 2)),
            pltpu.SemaphoreType.DMA((2, Z, 2)),
            pltpu.SemaphoreType.DMA((2,)),
            pltpu.SemaphoreType.DMA((2,)),
            pltpu.SemaphoreType.DMA((2,)),
            pltpu.SemaphoreType.DMA((2,)),
        ],
        compiler_params=pltpu.CompilerParams(
            collective_id=1, has_side_effects=True, vmem_limit_bytes=56 * 1024 * 1024
        ),
    )(tab, idx, x, vals)


def final_kernel(scale, f_ref, back_ref, w_ref, grad_ref, wg_ref, part, r1, a1, r2, a2, r3, r4, r5, *sems):
    s1, v1, s2, v2, s3, v3, s4, v4, s5, v5 = sems
    r, z, yc, c = place()
    peers_x = [(r, (c + d) % X) for d in range(1, X)]
    peers_y = [(z * YC + (yc + 1 + j) % YC, c) for j in range(YC - 1)]
    peers_z = [((z + 1 + i) % Z * YC + yc, c) for i in range(Z - 1)]
    greet(peers_x + peers_y + peers_z)
    width = w_ref.shape[0]
    share = width // X
    small = share // YC
    back = back_ref[...]
    high = back.astype(BF16)
    low = (back - high.astype(F32)).astype(BF16)
    contract = (((0,), (0,)), ((), ()))
    part[...] = lax.dot_general(f_ref[...], high, contract, preferred_element_type=F32) + lax.dot_general(
        f_ref[...], low, contract, preferred_element_type=F32
    )

    def share_of(d):
        return pl.ds(pl.multiple_of((c + d) % X * share, share), share)

    one = [remote(part.at[share_of(d)], r1.at[d - 1], s1.at[d - 1], v1.at[d - 1], peers_x[d - 1]) for d in range(1, X)]
    for copy in one:
        copy.start()
    grad_ref[...] = lax.dot_general(high, w_ref[...], (((1,), (1,)), ((), ())), preferred_element_type=F32).astype(BF16)
    for copy in one:
        copy.wait()
    a1[...] = (part[share_of(0)] + r1[0]) + (r1[1] + r1[2])

    def small_of(j):
        return pl.ds(pl.multiple_of((yc + 1 + j) % YC * small, small), small)

    two = [remote(a1.at[small_of(j)], r2.at[j], s2.at[j], v2.at[j], peers_y[j]) for j in range(YC - 1)]
    for copy in two:
        copy.start()
    for copy in two:
        copy.wait()
    total = a1[small_of(YC - 1)]
    for j in range(YC - 1):
        total = total + r2[j]
    a2[...] = total
    r3[z] = total
    three = [remote(a2, r3.at[z], s3.at[i], v3.at[i], peers_z[i]) for i in range(Z - 1)]
    for copy in three:
        copy.start()
    for i in range(Z - 1):
        remote(a2, r3.at[(z + Z - 1 - i) % Z], s3.at[i], v3.at[i], peers_z[i]).wait()
    total = r3[0]
    for i in range(1, Z):
        total = total + r3[i]
    r4[yc] = total * scale
    four = [remote(r4.at[yc], r4.at[yc], s4.at[j], v4.at[j], peers_y[j]) for j in range(YC - 1)]
    for copy in four:
        copy.start()
    for j in range(YC - 1):
        remote(r4.at[yc], r4.at[(yc + YC - 1 - j) % YC], s4.at[j], v4.at[j], peers_y[j]).wait()
    five = [remote(r4, r5.at[c], s5.at[d], v5.at[d], peers_x[d]) for d in range(X - 1)]
    for copy in five:
        copy.start()
    r5[c] = r4[...]
    for d in range(X - 1):
        remote(r4, r5.at[(c + X - 1 - d) % X], s5.at[d], v5.at[d], peers_x[d]).wait()
    wg_ref[...] = r5[...].reshape(width, width)


def finish(features, back, weight, node_total):
    rows, width = features.shape
    share = width // X
    small = share // YC
    vmem = pl.BlockSpec(memory_space=pltpu.VMEM)
    dma = lambda n: pltpu.SemaphoreType.DMA((n,))
    return pl.pallas_call(
        functools.partial(final_kernel, 1.0 / math.sqrt(node_total)),
        out_shape=(jax.ShapeDtypeStruct((rows, width), BF16), jax.ShapeDtypeStruct((width, width), F32)),
        in_specs=[vmem] * 3,
        out_specs=(vmem, vmem),
        scratch_shapes=[
            pltpu.VMEM((width, width), F32),
            pltpu.VMEM((X - 1, share, width), F32),
            pltpu.VMEM((share, width), F32),
            pltpu.VMEM((YC - 1, small, width), F32),
            pltpu.VMEM((small, width), F32),
            pltpu.VMEM((Z, small, width), F32),
            pltpu.VMEM((YC, small, width), F32),
            pltpu.VMEM((X, YC, small, width), F32),
        ]
        + [dma(X - 1)] * 2
        + [dma(YC - 1)] * 2
        + [dma(Z - 1)] * 2
        + [dma(YC - 1)] * 2
        + [dma(X - 1)] * 2,
        compiler_params=pltpu.CompilerParams(collective_id=2, has_side_effects=True),
    )(features, back, weight)


def silu_parts(summed):
    sigmoid_vals = jax.nn.sigmoid(summed)
    return (summed * sigmoid_vals, sigmoid_vals * (1.0 + summed * (1.0 - sigmoid_vals)))


def on_device(features, weight, block_cols, block_vals, out_grad):
    own_rows, width = features.shape
    r, z, yc, c = place()
    flat = block_cols[:, 0].reshape(-1)
    owners, places = flat // OWN, flat % OWN
    slot = (yc + YC - 1 - owners % YC) % YC * Z + (z + Z - owners // YC) % Z
    idx = jnp.where(owners == r, YC * Z + places, slot)
    groups = jnp.arange(LANES, dtype=jnp.int32)
    wanted = (owners[:, None] == groups[None, :]) & (owners != r)[:, None]
    table = jnp.sum(jnp.where(wanted, places[:, None], 0), axis=0)
    tab = exchange_tables(jnp.broadcast_to(table[None], (8, LANES)))[:, 0]
    vals = block_vals[:, 0]
    mixed = jnp.dot(features, weight, preferred_element_type=F32).astype(BF16)
    summed = spmm(tab, idx, mixed.reshape(OWN, B, width), vals).reshape(own_rows, width)
    values, slopes = silu_parts(summed)
    own_grad = lax.dynamic_slice_in_dim(out_grad, c * own_rows, own_rows, 0)
    masked = (own_grad.astype(F32) * slopes).astype(BF16)
    back = spmm(tab, idx, masked.reshape(OWN, B, width), vals).reshape(own_rows, width)
    input_grad, weight_grad = finish(features, back, weight, own_rows * Z * YC * X)
    return (values.astype(BF16), input_grad, weight_grad)


def solution(mesh):
    placed = (
        P(("rows", "rep"), None),
        P(),
        P("rows", "rep", None),
        P("rows", "rep", None, None, None),
        P("rows", None),
    )
    return jax.shard_map(
        on_device,
        mesh=mesh,
        in_specs=placed,
        out_specs=(P(("rows", "rep"), None), P(("rows", "rep"), None), P()),
        check_vma=False,
    )
```

```python
import functools
import math

import jax
import jax.numpy as jnp
from jax import lax
from jax.experimental import pallas as pl
from jax.experimental.pallas import tpu as pltpu
from jax.sharding import PartitionSpec as P

MESH = pl.DeviceIdType.MESH
Z = 8
YC = 8
X = 4
B = 128
LANES = 128
OWN = 8
F32 = jnp.float32
BF16 = jnp.bfloat16


def place():
    r, c = lax.axis_index("rows"), lax.axis_index("rep")
    return r, r // YC, r % YC, c


def greet(partners):
    barrier = pltpu.get_barrier_semaphore()
    for device in partners:
        pl.semaphore_signal(barrier, inc=1, device_id=device, device_id_type=MESH)
    pl.semaphore_wait(barrier, len(partners))


def remote(src, dst, send, recv, device):
    return pltpu.make_async_remote_copy(
        src_ref=src, dst_ref=dst, send_sem=send, recv_sem=recv, device_id=device, device_id_type=MESH
    )


def wait_bytes(ref, sem):
    pltpu.make_async_copy(ref, ref, sem).wait()


def layer_kernel(
    scale, own_tab, idx, f_ref, w_ref, vals_hbm, grad_hbm, act_ref, ig_ref, wg_ref, *scratch
):
    ag = [scratch[n * Z : (n + 1) * Z] for n in range(4)]
    at = 4 * Z
    sbuf, src, xs, xr, own = (scratch[at + 4 * i : at + 4 * i + 4] for i in range(5))
    at += 20
    (got, tab, vals, grad, ft, high, ig_acc, part, r1, a1, r2, a2, r3, r4, r5) = scratch[at : at + 15]
    at += 15
    (t_send, t_recv, l_sem, z_send, z_recv, y_send, y_recv, x_send, x_recv) = scratch[at : at + 9]
    s1, v1, s2, v2, s3, v3, s4, v4, s5, v5 = scratch[at + 9 :]
    r, z, yc, c = place()
    half = OWN // 2
    peers_x = [(r, (c + d) % X) for d in range(1, X)]
    peers_y = [(z * YC + (yc + 1 + j) % YC, c) for j in range(YC - 1)]
    peers_z = [((z + 1 + i) % Z * YC + yc, c) for i in range(Z - 1)]
    up, down = peers_z[0], peers_z[Z - 2]

    load_vals = pltpu.make_async_copy(vals_hbm, vals, l_sem.at[0])
    load_grad = pltpu.make_async_copy(grad_hbm.at[pl.ds(c * OWN, OWN)], grad, l_sem.at[1])
    load_vals.start()
    load_grad.start()

    def columns(h):
        return pl.ds(h * LANES, LANES)

    def mix(h):
        def row(p, _):
            ag[h][0][p] = jnp.dot(f_ref[p], w_ref[:, columns(h)], preferred_element_type=F32).astype(BF16)
            return 0

        lax.fori_loop(0, OWN, row, 0)

    mix(0)
    greet(peers_x + peers_y + peers_z)

    def hop(n, k, forward):
        nxt = (k + 1) % Z if forward else (k - 1) % Z
        source, target = ag[n][k], ag[n][nxt]
        lane = 0 if forward else 1
        if nxt == Z // 2:
            rows = pl.ds(0, half) if forward else pl.ds(half, half)
            source, target = source.at[rows], target.at[rows]
        return remote(source, target, z_send.at[n, nxt, lane], z_recv.at[n, nxt, lane], up if forward else down)

    def arrived(n, k, lane):
        if k == Z // 2:
            chunk = ag[n][k].at[pl.ds(0 if lane == 0 else half, half)]
        else:
            chunk = ag[n][k]
        wait_bytes(chunk, z_recv.at[n, k, lane])

    def serve(n, k):
        column = (z - k + Z) % Z * YC + yc

        def pick(j, _):
            sbuf[n][j * Z + k] = ag[n][k][tab[YC - 2 - j, column]]
            return 0

        lax.fori_loop(0, YC - 1, pick, 0)
        if k == 0:
            for p in range(OWN):
                src[n][YC * Z + p] = ag[n][0][p]
        else:
            src[n][(YC - 1) * Z + k] = ag[n][k][tab[YC - 1, column]]

        def post(j, _):
            slot = j * Z + k
            target = (z * YC + (yc + 1 + j) % YC, c)
            remote(sbuf[n].at[slot], src[n].at[slot], y_send.at[n], y_recv.at[n], target).start()
            return 0

        lax.fori_loop(0, YC - 1, post, 0)

    def products(n):
        wait_bytes(src[n].at[pl.ds(0, (YC - 1) * Z)], y_recv.at[n])
        for d in (2, 1, 3, 0):
            first = (c + d) % X * OWN

            def post(p):
                slot = (d - 1) * OWN + p
                remote(xs[n].at[slot], xr[n].at[slot], x_send.at[n], x_recv.at[n], (r, (c + d) % X)).start()

            def row(p, _):
                b = first + p
                total = jnp.dot(vals[b, 0], src[n][idx[2 * b]], preferred_element_type=F32)
                total += jnp.dot(vals[b, 1], src[n][idx[2 * b + 1]], preferred_element_type=F32)
                if d == 0:
                    own[n][p] = total
                else:
                    xs[n][(d - 1) * OWN + p] = total.astype(BF16)

                    @pl.when(p > 0)
                    def _():
                        post(p - 1)

                return 0

            lax.fori_loop(0, OWN, row, 0)
            if d != 0:
                post(OWN - 1)

    def summed(n, p):
        a, b, e = (xr[n][d * OWN + p].astype(F32) for d in range(X - 1))
        return (own[n][p] + a) + (b + e)

    def activate(h):
        wait_bytes(xr[h], x_recv.at[h])

        def row(p, _):
            value, slope = silu_parts(summed(h, p))
            act_ref[p, :, columns(h)] = value.astype(BF16)
            ag[2 + h][0][p] = (grad[p, :, columns(h)].astype(F32) * slope).astype(BF16)
            return 0

        lax.fori_loop(0, OWN, row, 0)

    def back(h):
        n = 2 + h
        wait_bytes(xr[n], x_recv.at[n])
        part[h] = jnp.zeros_like(part[h])

        def row(p, _):
            total = summed(n, p)
            top = total.astype(BF16)
            rest = (total - top.astype(F32)).astype(BF16)
            part[h] += jnp.dot(ft[p], top, preferred_element_type=F32) + jnp.dot(
                ft[p], rest, preferred_element_type=F32
            )
            high[h, p] = top
            return 0

        lax.fori_loop(0, OWN, row, 0)

    def input_term(h, p):
        return lax.dot_general(
            high[h, p], w_ref[:, columns(h)], (((1,), (1,)), ((), ())), preferred_element_type=F32
        )

    def ring(n, step):
        if step < Z // 2:
            arrived(n, step, 0)
            hop(n, step, True).start()
            arrived(n, Z - step, 1)
            hop(n, Z - step, False).start()
            serve(n, step)
            serve(n, Z - step)
        else:
            arrived(n, step, 0)
            arrived(n, step, 1)
            serve(n, step)

    def begin(n):
        hop(n, 0, True).start()
        hop(n, 0, False).start()

    begin(0)
    tables = [remote(own_tab, got.at[j], t_send.at[j], t_recv.at[j], peers_y[j]) for j in range(YC - 1)]
    for copy in tables:
        copy.start()
    mix(1)
    for copy in tables:
        copy.wait()
    rows = [got.at[j, 0] for j in range(YC - 1)] + [own_tab.at[0]]
    moves = [pltpu.make_async_copy(row, tab.at[j], l_sem.at[2 + j]) for j, row in enumerate(rows)]
    for move in moves:
        move.start()
    for move in moves:
        move.wait()

    serve(0, 0)
    ring(0, 1)
    begin(1)
    serve(1, 0)
    for p in range(OWN):
        ft[p] = f_ref[p].T
    ring(0, 2)
    ring(0, 3)
    ring(1, 1)
    ring(0, 4)
    load_vals.wait()
    load_grad.wait()
    products(0)
    ring(1, 2)
    ring(1, 3)
    activate(0)
    begin(2)
    serve(2, 0)
    ring(1, 4)
    products(1)
    ring(2, 1)
    ring(2, 2)
    activate(1)
    begin(3)
    serve(3, 0)
    ring(2, 3)
    ring(3, 1)
    ring(2, 4)
    products(2)
    ring(3, 2)
    ring(3, 3)
    back(0)
    ring(3, 4)
    products(3)

    def first_term(p, _):
        ig_acc[p] = input_term(0, p)
        return 0

    lax.fori_loop(0, OWN, first_term, 0)
    back(1)

    share = part.shape[1] // X
    small = share // YC

    def share_of(d):
        return pl.ds(pl.multiple_of((c + d) % X * share, share), share)

    def small_of(j):
        return pl.ds(pl.multiple_of((yc + 1 + j) % YC * small, small), small)

    one = [
        remote(part.at[:, share_of(d)], r1.at[d - 1], s1.at[d - 1], v1.at[d - 1], peers_x[d - 1]) for d in range(1, X)
    ]
    for copy in one:
        copy.start()

    def second_term(p, _):
        ig_ref[p] = (ig_acc[p] + input_term(1, p)).astype(BF16)
        return 0

    lax.fori_loop(0, OWN, second_term, 0)
    for copy in one:
        copy.wait()
    a1[...] = (part[:, share_of(0)] + r1[0]) + (r1[1] + r1[2])
    two = [remote(a1.at[:, small_of(j)], r2.at[j], s2.at[j], v2.at[j], peers_y[j]) for j in range(YC - 1)]
    for copy in two:
        copy.start()
    for copy in two:
        copy.wait()
    total = a1[:, small_of(YC - 1)]
    for j in range(YC - 1):
        total = total + r2[j]
    a2[...] = total
    r3[z] = total
    three = [remote(a2, r3.at[z], s3.at[i], v3.at[i], peers_z[i]) for i in range(Z - 1)]
    for copy in three:
        copy.start()
    for i in range(Z - 1):
        remote(a2, r3.at[(z + Z - 1 - i) % Z], s3.at[i], v3.at[i], peers_z[i]).wait()
    total = r3[0]
    for i in range(1, Z):
        total = total + r3[i]
    r4[yc] = total * scale
    four = [remote(r4.at[yc], r4.at[yc], s4.at[j], v4.at[j], peers_y[j]) for j in range(YC - 1)]
    for copy in four:
        copy.start()
    for j in range(YC - 1):
        remote(r4.at[yc], r4.at[(yc + YC - 1 - j) % YC], s4.at[j], v4.at[j], peers_y[j]).wait()
    five = [remote(r4, r5.at[c], s5.at[d], v5.at[d], peers_x[d]) for d in range(X - 1)]
    for copy in five:
        copy.start()
    r5[c] = r4[...]
    for d in range(X - 1):
        remote(r4, r5.at[(c + X - 1 - d) % X], s5.at[d], v5.at[d], peers_x[d]).wait()
    for q in range(X):
        for j in range(YC):
            for h in range(2):
                wg_ref[pl.ds((q * YC + j) * small, small), columns(h)] = r5[q, j, h]

    for n in range(4):
        for k in range(Z // 2):
            hop(n, k, True).wait_send()
            hop(n, (Z - k) % Z, False).wait_send()
        wait_bytes(sbuf[n], y_send.at[n])
        wait_bytes(xs[n], x_send.at[n])


def layer(own_tab, idx, features, weight, vals, out_grad, node_total):
    width = weight.shape[0]
    share = width // X
    small = share // YC
    blocks = lambda n, kind: pltpu.VMEM((n, B, LANES), kind)
    smem = pl.BlockSpec(memory_space=pltpu.SMEM)
    vmem = pl.BlockSpec(memory_space=pltpu.VMEM)
    hbm = pl.BlockSpec(memory_space=pl.ANY)
    dma = lambda *shape: pltpu.SemaphoreType.DMA(shape)
    wide = jax.ShapeDtypeStruct(features.shape, BF16)
    return pl.pallas_call(
        functools.partial(layer_kernel, 1.0 / math.sqrt(node_total)),
        out_shape=(wide, wide, jax.ShapeDtypeStruct((width, width), F32)),
        in_specs=[vmem, smem, vmem, vmem, hbm, hbm],
        out_specs=(vmem, vmem, vmem),
        scratch_shapes=[blocks(OWN, BF16) for _ in range(4 * Z)]
        + [blocks((YC - 1) * Z, BF16)] * 4
        + [blocks(YC * Z + OWN, BF16)] * 4
        + [blocks((X - 1) * OWN, BF16)] * 8
        + [blocks(OWN, F32)] * 4
        + [
            pltpu.VMEM((YC - 1, 8, LANES), jnp.int32),
            pltpu.SMEM((YC, LANES), jnp.int32),
            pltpu.VMEM(vals.shape, BF16),
            pltpu.VMEM(features.shape, BF16),
            pltpu.VMEM((OWN, width, B), BF16),
            pltpu.VMEM((2, OWN, B, LANES), BF16),
            pltpu.VMEM((OWN, B, width), F32),
            pltpu.VMEM((2, width, LANES), F32),
            pltpu.VMEM((X - 1, 2, share, LANES), F32),
            pltpu.VMEM((2, share, LANES), F32),
            pltpu.VMEM((YC - 1, 2, small, LANES), F32),
            pltpu.VMEM((2, small, LANES), F32),
            pltpu.VMEM((Z, 2, small, LANES), F32),
            pltpu.VMEM((YC, 2, small, LANES), F32),
            pltpu.VMEM((X, YC, 2, small, LANES), F32),
        ]
        + [dma(YC - 1), dma(YC - 1), dma(2 + YC), dma(4, Z, 2), dma(4, Z, 2), dma(4), dma(4), dma(4), dma(4)]
        + [dma(X - 1)] * 2
        + [dma(YC - 1)] * 2
        + [dma(Z - 1)] * 2
        + [dma(YC - 1)] * 2
        + [dma(X - 1)] * 2,
        compiler_params=pltpu.CompilerParams(
            collective_id=0, has_side_effects=True, vmem_limit_bytes=60 * 1024 * 1024
        ),
    )(own_tab, idx, features, weight, vals, out_grad)


def silu_parts(summed):
    sigmoid_vals = jax.nn.sigmoid(summed)
    return (summed * sigmoid_vals, sigmoid_vals * (1.0 + summed * (1.0 - sigmoid_vals)))


def on_device(features, weight, block_cols, block_vals, out_grad):
    own_rows, width = features.shape
    r, z, yc, c = place()
    flat = block_cols[:, 0].reshape(-1)
    owners, places = flat // OWN, flat % OWN
    slot = (yc + YC - 1 - owners % YC) % YC * Z + (z + Z - owners // YC) % Z
    idx = jnp.where(owners == r, YC * Z + places, slot)
    groups = jnp.arange(LANES, dtype=jnp.int32)
    wanted = (owners[:, None] == groups[None, :]) & (owners != r)[:, None]
    table = jnp.sum(jnp.where(wanted, places[:, None], 0), axis=0)
    own_tab = jnp.broadcast_to(table[None], (8, LANES))
    activations, input_grad, weight_grad = layer(
        own_tab,
        idx,
        features.reshape(OWN, B, width),
        weight,
        block_vals[:, 0],
        out_grad.reshape(-1, B, width),
        own_rows * Z * YC * X,
    )
    return (activations.reshape(own_rows, width), input_grad.reshape(own_rows, width), weight_grad)


def solution(mesh):
    placed = (
        P(("rows", "rep"), None),
        P(),
        P("rows", "rep", None),
        P("rows", "rep", None, None, None),
        P("rows", None),
    )
    return jax.shard_map(
        on_device,
        mesh=mesh,
        in_specs=placed,
        out_specs=(P(("rows", "rep"), None), P(("rows", "rep"), None), P()),
        check_vma=False,
    )
```

```python
import functools
import math

import jax
import jax.numpy as jnp
from jax import lax
from jax.experimental import pallas as pl
from jax.experimental.pallas import tpu as pltpu
from jax.sharding import PartitionSpec as P

MESH = pl.DeviceIdType.MESH
Z = 8
YC = 8
X = 4
B = 128
LANES = 128
OWN = 8
F32 = jnp.float32
BF16 = jnp.bfloat16


def place():
    r, c = lax.axis_index("rows"), lax.axis_index("rep")
    return r, r // YC, r % YC, c


def greet(partners):
    for device in partners:
        pl.semaphore_signal(pltpu.get_barrier_semaphore(), inc=1, device_id=device, device_id_type=MESH)


def remote(src, dst, send, recv, device):
    return pltpu.make_async_remote_copy(
        src_ref=src, dst_ref=dst, send_sem=send, recv_sem=recv, device_id=device, device_id_type=MESH
    )


def wait_bytes(ref, sem):
    pltpu.make_async_copy(ref, ref, sem).wait()


def layer_kernel(
    scale, own_tab, idx, f_hbm, w_ref, vals_hbm, grad_hbm, act_hbm, ig_hbm, wg_ref, *scratch
):
    ag = [scratch[n * Z : (n + 1) * Z] for n in range(4)]
    at = 4 * Z
    sbuf, src, xs, xr, own = (scratch[at + 4 * i : at + 4 * i + 4] for i in range(5))
    at += 20
    (got, tab, f_ref, act_ref, ig_ref, vals, grad, ft, high, ig_acc, part) = scratch[at : at + 11]
    (r1, a1, r2, a2, r3, r4, r5) = scratch[at + 11 : at + 18]
    at += 18
    (t_send, t_recv, l_sem, z_send, z_recv, y_send, y_recv, x_send, x_recv) = scratch[at : at + 9]
    s1, v1, s2, v2, s3, v3, s4, v4, s5, v5 = scratch[at + 9 :]
    r, z, yc, c = place()
    half = OWN // 2
    peers_x = [(r, (c + d) % X) for d in range(1, X)]
    peers_y = [(z * YC + (yc + 1 + j) % YC, c) for j in range(YC - 1)]
    peers_z = [((z + 1 + i) % Z * YC + yc, c) for i in range(Z - 1)]
    up, down = peers_z[0], peers_z[Z - 2]

    load_features = pltpu.make_async_copy(f_hbm, f_ref, l_sem.at[2])
    load_features.start()
    greet(peers_x + peers_y + peers_z)
    load_grad = pltpu.make_async_copy(grad_hbm.at[pl.ds(c * OWN, OWN)], grad, l_sem.at[1])
    load_vals = [
        pltpu.make_async_copy(vals_hbm.at[:, s], vals.at[:, :, pl.ds(s * B, B)], l_sem.at[3 * s]) for s in range(2)
    ]
    save_act = pltpu.make_async_copy(act_ref, act_hbm, l_sem.at[4])
    save_ig = pltpu.make_async_copy(ig_ref, ig_hbm, l_sem.at[5])

    def columns(h):
        return pl.ds(h * LANES, LANES)

    def mix(h):
        def row(p, _):
            ag[h][0][p] = jnp.dot(f_ref[p], w_ref[:, columns(h)], preferred_element_type=F32).astype(BF16)
            return 0

        lax.fori_loop(0, OWN, row, 0)

    load_features.wait()
    mix(0)
    pl.semaphore_wait(pltpu.get_barrier_semaphore(), X + YC + Z - 3)

    def hop(n, k, forward):
        nxt = (k + 1) % Z if forward else (k - 1) % Z
        source, target = ag[n][k], ag[n][nxt]
        lane = 0 if forward else 1
        if nxt == Z // 2:
            rows = pl.ds(0, half) if forward else pl.ds(half, half)
            source, target = source.at[rows], target.at[rows]
        return remote(source, target, z_send.at[n, nxt, lane], z_recv.at[n, nxt, lane], up if forward else down)

    def arrived(n, k, lane):
        if k == Z // 2:
            chunk = ag[n][k].at[pl.ds(0 if lane == 0 else half, half)]
        else:
            chunk = ag[n][k]
        wait_bytes(chunk, z_recv.at[n, k, lane])

    def serve(n, k):
        column = (z - k + Z) % Z * YC + yc

        def pick(j, _):
            sbuf[n][j * Z + k] = ag[n][k][tab[YC - 2 - j, column]]
            return 0

        lax.fori_loop(0, YC - 1, pick, 0)
        if k == 0:
            for p in range(OWN):
                src[n][YC * Z + p] = ag[n][0][p]
        else:
            src[n][(YC - 1) * Z + k] = ag[n][k][tab[YC - 1, column]]

        def post(j, _):
            slot = j * Z + k
            target = (z * YC + (yc + 1 + j) % YC, c)
            remote(sbuf[n].at[slot], src[n].at[slot], y_send.at[n], y_recv.at[n], target).start()
            return 0

        lax.fori_loop(0, YC - 1, post, 0)

    def products(n, classes):
        for d in classes:
            first = (c + d) % X * OWN

            def pair(q, _):
                totals = []
                for p in (2 * q, 2 * q + 1):
                    b = first + p
                    used = jnp.concatenate([src[n][idx[2 * b]], src[n][idx[2 * b + 1]]], axis=0)
                    totals.append(jnp.dot(vals[b], used, preferred_element_type=F32))
                if d == 0:
                    own[n][2 * q], own[n][2 * q + 1] = totals
                else:
                    at = (d - 1) * OWN + 2 * q
                    xs[n][at], xs[n][at + 1] = [total.astype(BF16) for total in totals]
                    both = pl.ds(at, 2)
                    target = (r, (c + d) % X)
                    remote(xs[n].at[both], xr[n].at[both], x_send.at[n], x_recv.at[n], target).start()
                return 0

            lax.fori_loop(0, OWN // 2, pair, 0)

    def gathered(n):
        wait_bytes(src[n].at[pl.ds(0, (YC - 1) * Z)], y_recv.at[n])

    def summed(n, p):
        a, b, e = (xr[n][d * OWN + p].astype(F32) for d in range(X - 1))
        return (own[n][p] + a) + (b + e)

    def activate(h):
        wait_bytes(xr[h], x_recv.at[h])

        def row(p, _):
            value, slope = silu_parts(summed(h, p))
            act_ref[p, :, columns(h)] = value.astype(BF16)
            ag[2 + h][0][p] = (grad[p, :, columns(h)].astype(F32) * slope).astype(BF16)
            return 0

        lax.fori_loop(0, OWN, row, 0)

    def back(h):
        n = 2 + h
        wait_bytes(xr[n], x_recv.at[n])
        part[h] = jnp.zeros_like(part[h])

        def row(p, _):
            total = summed(n, p)
            top = total.astype(BF16)
            rest = (total - top.astype(F32)).astype(BF16)
            part[h] += jnp.dot(ft[p], top, preferred_element_type=F32) + jnp.dot(
                ft[p], rest, preferred_element_type=F32
            )
            high[h, p] = top
            return 0

        lax.fori_loop(0, OWN, row, 0)

    def input_term(h, p):
        return lax.dot_general(
            high[h, p], w_ref[:, columns(h)], (((1,), (1,)), ((), ())), preferred_element_type=F32
        )

    def ring(n, step):
        if step < Z // 2:
            arrived(n, step, 0)
            hop(n, step, True).start()
            arrived(n, Z - step, 1)
            hop(n, Z - step, False).start()
            serve(n, step)
            serve(n, Z - step)
        else:
            arrived(n, step, 0)
            arrived(n, step, 1)
            serve(n, step)

    def begin(n):
        hop(n, 0, True).start()
        hop(n, 0, False).start()

    begin(0)
    tables = [remote(own_tab, got.at[j], t_send.at[j], t_recv.at[j], peers_y[j]) for j in range(YC - 1)]
    for copy in tables:
        copy.start()
    load_grad.start()
    for load in load_vals:
        load.start()
    mix(1)
    for copy in tables:
        copy.wait()
    rows = [got.at[j, 0] for j in range(YC - 1)] + [own_tab.at[0]]
    moves = [pltpu.make_async_copy(row, tab.at[j], l_sem.at[6 + j]) for j, row in enumerate(rows)]
    for move in moves:
        move.start()
    for move in moves:
        move.wait()

    serve(0, 0)
    serve(1, 0)
    for p in range(OWN):
        ft[p] = f_ref[p].T
    ring(0, 1)
    ring(0, 2)
    ring(0, 3)
    begin(1)
    ring(0, 4)
    load_grad.wait()
    for load in load_vals:
        load.wait()
    ring(1, 1)
    gathered(0)
    products(0, (2, 1))
    ring(1, 2)
    products(0, (3, 0))
    ring(1, 3)
    activate(0)
    begin(2)
    ring(1, 4)
    serve(2, 0)
    gathered(1)
    products(1, (2, 1))
    ring(2, 1)
    products(1, (3, 0))
    ring(2, 2)
    activate(1)
    save_act.start()
    serve(3, 0)
    ring(2, 3)
    begin(3)
    ring(2, 4)
    ring(3, 1)
    gathered(2)
    products(2, (2, 1))
    ring(3, 2)
    products(2, (3, 0))
    ring(3, 3)
    ring(3, 4)
    back(0)

    def first_term(p, _):
        ig_acc[p] = input_term(0, p)
        return 0

    lax.fori_loop(0, OWN, first_term, 0)
    gathered(3)
    products(3, (2, 1, 3, 0))
    back(1)

    share = part.shape[1] // X
    small = share // YC

    def share_of(d):
        return pl.ds(pl.multiple_of((c + d) % X * share, share), share)

    def small_of(j):
        return pl.ds(pl.multiple_of((yc + 1 + j) % YC * small, small), small)

    one = [
        remote(part.at[:, share_of(d)], r1.at[d - 1], s1.at[d - 1], v1.at[d - 1], peers_x[d - 1]) for d in range(1, X)
    ]
    for copy in one:
        copy.start()

    def second_term(p, _):
        ig_ref[p] = (ig_acc[p] + input_term(1, p)).astype(BF16)
        return 0

    lax.fori_loop(0, OWN, second_term, 0)
    save_ig.start()
    for copy in one:
        copy.wait()
    a1[...] = (part[:, share_of(0)] + r1[0]) + (r1[1] + r1[2])
    two = [remote(a1.at[:, small_of(j)], r2.at[j], s2.at[j], v2.at[j], peers_y[j]) for j in range(YC - 1)]
    for copy in two:
        copy.start()
    for copy in two:
        copy.wait()
    total = a1[:, small_of(YC - 1)]
    for j in range(YC - 1):
        total = total + r2[j]
    a2[...] = total
    r3[z] = total
    three = [remote(a2, r3.at[z], s3.at[i], v3.at[i], peers_z[i]) for i in range(Z - 1)]
    for copy in three:
        copy.start()
    for i in range(Z - 1):
        remote(a2, r3.at[(z + Z - 1 - i) % Z], s3.at[i], v3.at[i], peers_z[i]).wait()
    total = r3[0]
    for i in range(1, Z):
        total = total + r3[i]
    r4[yc] = total * scale
    four = [remote(r4.at[yc], r4.at[yc], s4.at[j], v4.at[j], peers_y[j]) for j in range(YC - 1)]
    for copy in four:
        copy.start()
    for j in range(YC - 1):
        remote(r4.at[yc], r4.at[(yc + YC - 1 - j) % YC], s4.at[j], v4.at[j], peers_y[j]).wait()
    five = [remote(r4, r5.at[c], s5.at[d], v5.at[d], peers_x[d]) for d in range(X - 1)]
    for copy in five:
        copy.start()
    r5[c] = r4[...]
    for d in range(X - 1):
        remote(r4, r5.at[(c + X - 1 - d) % X], s5.at[d], v5.at[d], peers_x[d]).wait()
    for q in range(X):
        for j in range(YC):
            for h in range(2):
                wg_ref[pl.ds((q * YC + j) * small, small), columns(h)] = r5[q, j, h]

    save_act.wait()
    save_ig.wait()
    for n in range(4):
        for k in range(Z // 2):
            hop(n, k, True).wait_send()
            hop(n, (Z - k) % Z, False).wait_send()
        wait_bytes(sbuf[n], y_send.at[n])
        wait_bytes(xs[n], x_send.at[n])


def layer(own_tab, idx, features, weight, vals, out_grad, node_total):
    width = weight.shape[0]
    share = width // X
    small = share // YC
    blocks = lambda n, kind: pltpu.VMEM((n, B, LANES), kind)
    smem = pl.BlockSpec(memory_space=pltpu.SMEM)
    vmem = pl.BlockSpec(memory_space=pltpu.VMEM)
    hbm = pl.BlockSpec(memory_space=pl.ANY)
    dma = lambda *shape: pltpu.SemaphoreType.DMA(shape)
    wide = jax.ShapeDtypeStruct(features.shape, BF16)
    return pl.pallas_call(
        functools.partial(layer_kernel, 1.0 / math.sqrt(node_total)),
        out_shape=(wide, wide, jax.ShapeDtypeStruct((width, width), F32)),
        in_specs=[vmem, smem, hbm, vmem, hbm, hbm],
        out_specs=(hbm, hbm, vmem),
        scratch_shapes=[blocks(OWN, BF16) for _ in range(4 * Z)]
        + [blocks((YC - 1) * Z, BF16)] * 4
        + [blocks(YC * Z + OWN, BF16)] * 4
        + [blocks((X - 1) * OWN, BF16)] * 8
        + [blocks(OWN, F32)] * 4
        + [
            pltpu.VMEM((YC - 1, 8, LANES), jnp.int32),
            pltpu.SMEM((YC, LANES), jnp.int32),
            pltpu.VMEM(features.shape, BF16),
            pltpu.VMEM(features.shape, BF16),
            pltpu.VMEM(features.shape, BF16),
            pltpu.VMEM((vals.shape[0], B, 2 * B), BF16),
            pltpu.VMEM(features.shape, BF16),
            pltpu.VMEM((OWN, width, B), BF16),
            pltpu.VMEM((2, OWN, B, LANES), BF16),
            pltpu.VMEM((OWN, B, width), F32),
            pltpu.VMEM((2, width, LANES), F32),
            pltpu.VMEM((X - 1, 2, share, LANES), F32),
            pltpu.VMEM((2, share, LANES), F32),
            pltpu.VMEM((YC - 1, 2, small, LANES), F32),
            pltpu.VMEM((2, small, LANES), F32),
            pltpu.VMEM((Z, 2, small, LANES), F32),
            pltpu.VMEM((YC, 2, small, LANES), F32),
            pltpu.VMEM((X, YC, 2, small, LANES), F32),
        ]
        + [dma(YC - 1), dma(YC - 1), dma(6 + YC), dma(4, Z, 2), dma(4, Z, 2), dma(4), dma(4), dma(4), dma(4)]
        + [dma(X - 1)] * 2
        + [dma(YC - 1)] * 2
        + [dma(Z - 1)] * 2
        + [dma(YC - 1)] * 2
        + [dma(X - 1)] * 2,
        compiler_params=pltpu.CompilerParams(
            collective_id=0, has_side_effects=True, vmem_limit_bytes=60 * 1024 * 1024
        ),
    )(own_tab, idx, features, weight, vals, out_grad)


def silu_parts(summed):
    sigmoid_vals = jax.nn.sigmoid(summed)
    return (summed * sigmoid_vals, sigmoid_vals * (1.0 + summed * (1.0 - sigmoid_vals)))


def on_device(features, weight, block_cols, block_vals, out_grad):
    own_rows, width = features.shape
    r, z, yc, c = place()
    flat = block_cols[:, 0].reshape(-1)
    owners, places = flat // OWN, flat % OWN
    slot = (yc + YC - 1 - owners % YC) % YC * Z + (z + Z - owners // YC) % Z
    idx = jnp.where(owners == r, YC * Z + places, slot)
    groups = jnp.arange(LANES, dtype=jnp.int32)
    wanted = (owners[:, None] == groups[None, :]) & (owners != r)[:, None]
    table = jnp.sum(jnp.where(wanted, places[:, None], 0), axis=0)
    own_tab = jnp.broadcast_to(table[None], (8, LANES))
    activations, input_grad, weight_grad = layer(
        own_tab,
        idx,
        features.reshape(OWN, B, width),
        weight,
        block_vals[:, 0],
        out_grad.reshape(-1, B, width),
        own_rows * Z * YC * X,
    )
    return (activations.reshape(own_rows, width), input_grad.reshape(own_rows, width), weight_grad)


def solution(mesh):
    placed = (
        P(("rows", "rep"), None),
        P(),
        P("rows", "rep", None),
        P("rows", "rep", None, None, None),
        P("rows", None),
    )
    return jax.shard_map(
        on_device,
        mesh=mesh,
        in_specs=placed,
        out_specs=(P(("rows", "rep"), None), P(("rows", "rep"), None), P()),
        check_vma=False,
    )
```

```python
import functools
import math

import jax
import jax.numpy as jnp
from jax import lax
from jax.experimental import pallas as pl
from jax.experimental.pallas import tpu as pltpu
from jax.sharding import PartitionSpec as P

MESH = pl.DeviceIdType.MESH
Z = 8
YC = 8
X = 4
B = 128
LANES = 128
OWN = 8
PLANE = X * YC
F32 = jnp.float32
BF16 = jnp.bfloat16


def place():
    r, c = lax.axis_index("rows"), lax.axis_index("rep")
    return r, r // YC, r % YC, c


def greet(device):
    pl.semaphore_signal(pltpu.get_barrier_semaphore(), inc=1, device_id=device, device_id_type=MESH)


def remote(src, dst, send, recv, device):
    return pltpu.make_async_remote_copy(
        src_ref=src, dst_ref=dst, send_sem=send, recv_sem=recv, device_id=device, device_id_type=MESH
    )


def wait_bytes(ref, sem):
    pltpu.make_async_copy(ref, ref, sem).wait()


def layer_kernel(
    scale, own_tab, idx, f_hbm, w_ref, vals_hbm, grad_hbm, act_hbm, ig_hbm, wg_ref, *scratch
):
    ag = [scratch[n * Z : (n + 1) * Z] for n in range(4)]
    at = 4 * Z
    sbuf, src, xs, xr, own = (scratch[at + 4 * i : at + 4 * i + 4] for i in range(5))
    at += 20
    (got, tab, f_ref, act_ref, ig_ref, vals, grad, ft, high, parts, part, r1, a2, r3, r4) = scratch[at : at + 15]
    at += 15
    (t_send, t_recv, l_sem, z_send, z_recv, y_send, y_recv, x_send, x_recv) = scratch[at : at + 9]
    s1, v1, s2, v2, s3, v3 = scratch[at + 9 :]
    r, z, yc, c = place()
    half = OWN // 2
    rank = c * YC + yc
    small = part.shape[1] // PLANE
    peers_y = [(z * YC + (yc + 1 + j) % YC, c) for j in range(YC - 1)]
    peers_z = [((z + 1 + i) % Z * YC + yc, c) for i in range(Z - 1)]
    up, down = peers_z[0], peers_z[Z - 2]

    load_features = pltpu.make_async_copy(f_hbm, f_ref, l_sem.at[2])
    load_features.start()

    def in_plane(j):
        t = (rank + j) % PLANE
        return (z * YC + t % YC, t // YC), t

    def greet_plane(j, _):
        greet(in_plane(j)[0])
        return 0

    for device in peers_z:
        greet(device)
    lax.fori_loop(1, PLANE, greet_plane, 0)
    load_grad = pltpu.make_async_copy(grad_hbm.at[pl.ds(c * OWN, OWN)], grad, l_sem.at[1])
    load_vals = [
        pltpu.make_async_copy(vals_hbm.at[:, s], vals.at[:, :, pl.ds(s * B, B)], l_sem.at[3 * s]) for s in range(2)
    ]
    save_act = pltpu.make_async_copy(act_ref, act_hbm, l_sem.at[4])
    save_ig = pltpu.make_async_copy(ig_ref, ig_hbm, l_sem.at[5])

    def columns(h):
        return pl.ds(h * LANES, LANES)

    def mix(h):
        mixed = jnp.dot(f_ref[...].reshape(-1, f_ref.shape[2]), w_ref[:, columns(h)], preferred_element_type=F32)
        ag[h][0][...] = mixed.astype(BF16).reshape(OWN, B, LANES)

    load_features.wait()
    mix(0)
    pl.semaphore_wait(pltpu.get_barrier_semaphore(), PLANE + Z - 2)

    def hop(n, k, forward):
        nxt = (k + 1) % Z if forward else (k - 1) % Z
        source, target = ag[n][k], ag[n][nxt]
        lane = 0 if forward else 1
        if nxt == Z // 2:
            rows = pl.ds(0, half) if forward else pl.ds(half, half)
            source, target = source.at[rows], target.at[rows]
        return remote(source, target, z_send.at[n, nxt, lane], z_recv.at[n, nxt, lane], up if forward else down)

    def arrived(n, k, lane):
        if k == Z // 2:
            chunk = ag[n][k].at[pl.ds(0 if lane == 0 else half, half)]
        else:
            chunk = ag[n][k]
        wait_bytes(chunk, z_recv.at[n, k, lane])

    def serve(n, k):
        column = (z - k + Z) % Z * YC + yc

        def pick(j, _):
            sbuf[n][j * Z + k] = ag[n][k][tab[YC - 2 - j, column]]
            return 0

        lax.fori_loop(0, YC - 1, pick, 0)
        if k == 0:
            for p in range(OWN):
                src[n][YC * Z + p] = ag[n][0][p]
        else:
            src[n][(YC - 1) * Z + k] = ag[n][k][tab[YC - 1, column]]

        def post(j, _):
            slot = j * Z + k
            target = (z * YC + (yc + 1 + j) % YC, c)
            remote(sbuf[n].at[slot], src[n].at[slot], y_send.at[n], y_recv.at[n], target).start()
            return 0

        lax.fori_loop(0, YC - 1, post, 0)

    def products(n, classes):
        for d in classes:
            first = (c + d) % X * OWN

            def pair(q, _):
                totals = []
                for p in (2 * q, 2 * q + 1):
                    b = first + p
                    used = jnp.concatenate([src[n][idx[2 * b]], src[n][idx[2 * b + 1]]], axis=0)
                    totals.append(jnp.dot(vals[b], used, preferred_element_type=F32))
                if d == 0:
                    own[n][2 * q], own[n][2 * q + 1] = totals
                else:
                    at = (d - 1) * OWN + 2 * q
                    xs[n][at], xs[n][at + 1] = [total.astype(BF16) for total in totals]
                    both = pl.ds(at, 2)
                    target = (r, (c + d) % X)
                    remote(xs[n].at[both], xr[n].at[both], x_send.at[n], x_recv.at[n], target).start()
                return 0

            lax.fori_loop(0, OWN // 2, pair, 0)

    def gathered(n):
        wait_bytes(src[n].at[pl.ds(0, (YC - 1) * Z)], y_recv.at[n])

    def summed(n, p):
        a, b, e = (xr[n][d * OWN + p].astype(F32) for d in range(X - 1))
        return (own[n][p] + a) + (b + e)

    def activate(h):
        wait_bytes(xr[h], x_recv.at[h])

        def row(p, _):
            value, slope = silu_parts(summed(h, p))
            act_ref[p, :, columns(h)] = value.astype(BF16)
            ag[2 + h][0][p] = (grad[p, :, columns(h)].astype(F32) * slope).astype(BF16)
            return 0

        lax.fori_loop(0, OWN, row, 0)

    def back(h):
        n = 2 + h
        wait_bytes(xr[n], x_recv.at[n])

        def row(p, _):
            nodes = pl.ds(pl.multiple_of(p * B, B), B)
            total = summed(n, p)
            top = total.astype(BF16)
            high[nodes, columns(h)] = top
            parts[nodes, columns(0)] = top
            parts[nodes, columns(1)] = (total - top.astype(F32)).astype(BF16)
            return 0

        lax.fori_loop(0, OWN, row, 0)
        both = jnp.dot(ft[...], parts[...], preferred_element_type=F32)
        part[h] = both[:, :LANES] + both[:, LANES:]

    def share_of(h, t):
        return part.at[h, pl.ds(pl.multiple_of(t * small, small), small)]

    def spread(h):
        def post(j, _):
            target, t = in_plane(j)
            remote(share_of(h, t), r1.at[h, j - 1], s1.at[h], v1.at[h], target).start()
            return 0

        lax.fori_loop(1, PLANE, post, 0)

    def collect(h):
        wait_bytes(r1.at[h], v1.at[h])
        total = share_of(h, rank)[...]
        for j in range(PLANE - 1):
            total = total + r1[h, j]
        a2[h] = total
        r3[h, z] = total
        for i in range(Z - 1):
            remote(a2.at[h], r3.at[h, z], s2.at[h, i], v2.at[h, i], peers_z[i]).start()

    def share(h):
        for i in range(Z - 1):
            remote(a2.at[h], r3.at[h, (z + Z - 1 - i) % Z], s2.at[h, i], v2.at[h, i], peers_z[i]).wait()
        total = r3[h, 0]
        for i in range(1, Z):
            total = total + r3[h, i]
        r4[h, rank] = total * scale

        def post(j, _):
            remote(r4.at[h, rank], r4.at[h, rank], s3.at[h], v3.at[h], in_plane(j)[0]).start()
            return 0

        lax.fori_loop(1, PLANE, post, 0)

    def finish(h):
        wait_bytes(r4.at[h, pl.ds(0, PLANE - 1)], v3.at[h])
        wg_ref[:, columns(h)] = r4[h].reshape(-1, LANES)

    def ring(n, step):
        if step < Z // 2:
            arrived(n, step, 0)
            hop(n, step, True).start()
            arrived(n, Z - step, 1)
            hop(n, Z - step, False).start()
            serve(n, step)
            serve(n, Z - step)
        else:
            arrived(n, step, 0)
            arrived(n, step, 1)
            serve(n, step)

    def begin(n):
        hop(n, 0, True).start()
        hop(n, 0, False).start()

    begin(0)
    tables = [remote(own_tab, got.at[j], t_send.at[j], t_recv.at[j], peers_y[j]) for j in range(YC - 1)]
    for copy in tables:
        copy.start()
    load_grad.start()
    for load in load_vals:
        load.start()
    mix(1)
    for copy in tables:
        copy.wait()
    rows = [got.at[j, 0] for j in range(YC - 1)] + [own_tab.at[0]]
    moves = [pltpu.make_async_copy(row, tab.at[j], l_sem.at[6 + j]) for j, row in enumerate(rows)]
    for move in moves:
        move.start()
    for move in moves:
        move.wait()

    serve(0, 0)
    serve(1, 0)
    for p in range(OWN):
        ft[:, p * B : (p + 1) * B] = f_ref[p].T
    ring(0, 1)
    ring(0, 2)
    ring(0, 3)
    begin(1)
    ring(0, 4)
    load_grad.wait()
    for load in load_vals:
        load.wait()
    ring(1, 1)
    gathered(0)
    products(0, (2, 1))
    ring(1, 2)
    products(0, (3, 0))
    ring(1, 3)
    activate(0)
    begin(2)
    ring(1, 4)
    serve(2, 0)
    gathered(1)
    products(1, (2, 1))
    ring(2, 1)
    products(1, (3, 0))
    ring(2, 2)
    activate(1)
    save_act.start()
    serve(3, 0)
    ring(2, 3)
    begin(3)
    ring(2, 4)
    ring(3, 1)
    gathered(2)
    products(2, (2, 1))
    ring(3, 2)
    products(2, (3, 0))
    ring(3, 3)
    ring(3, 4)
    back(0)

    spread(0)
    gathered(3)
    products(3, (2, 1))
    collect(0)
    products(3, (3, 0))
    share(0)
    back(1)
    spread(1)
    grads = lax.dot_general(high[...], w_ref[...], (((1,), (1,)), ((), ())), preferred_element_type=F32)
    ig_ref[...] = grads.astype(BF16).reshape(ig_ref.shape)
    save_ig.start()
    finish(0)
    collect(1)
    share(1)
    finish(1)

    save_act.wait()
    save_ig.wait()
    for h in range(2):
        wait_bytes(r1.at[h], s1.at[h])
        wait_bytes(r4.at[h, pl.ds(0, PLANE - 1)], s3.at[h])
    for n in range(4):
        for k in range(Z // 2):
            hop(n, k, True).wait_send()
            hop(n, (Z - k) % Z, False).wait_send()
        wait_bytes(sbuf[n], y_send.at[n])
        wait_bytes(xs[n], x_send.at[n])


def layer(own_tab, idx, features, weight, vals, out_grad, node_total):
    width = weight.shape[0]
    small = width // PLANE
    blocks = lambda n, kind: pltpu.VMEM((n, B, LANES), kind)
    smem = pl.BlockSpec(memory_space=pltpu.SMEM)
    vmem = pl.BlockSpec(memory_space=pltpu.VMEM)
    hbm = pl.BlockSpec(memory_space=pl.ANY)
    dma = lambda *shape: pltpu.SemaphoreType.DMA(shape)
    wide = jax.ShapeDtypeStruct(features.shape, BF16)
    return pl.pallas_call(
        functools.partial(layer_kernel, 1.0 / math.sqrt(node_total)),
        out_shape=(wide, wide, jax.ShapeDtypeStruct((width, width), F32)),
        in_specs=[vmem, smem, hbm, vmem, hbm, hbm],
        out_specs=(hbm, hbm, vmem),
        scratch_shapes=[blocks(OWN, BF16) for _ in range(4 * Z)]
        + [blocks((YC - 1) * Z, BF16)] * 4
        + [blocks(YC * Z + OWN, BF16)] * 4
        + [blocks((X - 1) * OWN, BF16)] * 8
        + [blocks(OWN, F32)] * 4
        + [
            pltpu.VMEM((YC - 1, 8, LANES), jnp.int32),
            pltpu.SMEM((YC, LANES), jnp.int32),
            pltpu.VMEM(features.shape, BF16),
            pltpu.VMEM(features.shape, BF16),
            pltpu.VMEM(features.shape, BF16),
            pltpu.VMEM((vals.shape[0], B, 2 * B), BF16),
            pltpu.VMEM(features.shape, BF16),
            pltpu.VMEM((width, OWN * B), BF16),
            pltpu.VMEM((OWN * B, width), BF16),
            pltpu.VMEM((OWN * B, 2 * LANES), BF16),
            pltpu.VMEM((2, width, LANES), F32),
            pltpu.VMEM((2, PLANE - 1, small, LANES), F32),
            pltpu.VMEM((2, small, LANES), F32),
            pltpu.VMEM((2, Z, small, LANES), F32),
            pltpu.VMEM((2, PLANE, small, LANES), F32),
        ]
        + [dma(YC - 1), dma(YC - 1), dma(6 + YC), dma(4, Z, 2), dma(4, Z, 2), dma(4), dma(4), dma(4), dma(4)]
        + [dma(2)] * 2
        + [dma(2, Z - 1)] * 2
        + [dma(2)] * 2,
        compiler_params=pltpu.CompilerParams(
            collective_id=0, has_side_effects=True, vmem_limit_bytes=60 * 1024 * 1024
        ),
    )(own_tab, idx, features, weight, vals, out_grad)


def silu_parts(summed):
    sigmoid_vals = jax.nn.sigmoid(summed)
    return (summed * sigmoid_vals, sigmoid_vals * (1.0 + summed * (1.0 - sigmoid_vals)))


def on_device(features, weight, block_cols, block_vals, out_grad):
    own_rows, width = features.shape
    r, z, yc, c = place()
    flat = block_cols[:, 0].reshape(-1)
    owners, places = flat // OWN, flat % OWN
    slot = (yc + YC - 1 - owners % YC) % YC * Z + (z + Z - owners // YC) % Z
    idx = jnp.where(owners == r, YC * Z + places, slot)
    groups = jnp.arange(LANES, dtype=jnp.int32)
    wanted = (owners[:, None] == groups[None, :]) & (owners != r)[:, None]
    table = jnp.sum(jnp.where(wanted, places[:, None], 0), axis=0)
    own_tab = jnp.broadcast_to(table[None], (8, LANES))
    activations, input_grad, weight_grad = layer(
        own_tab,
        idx,
        features.reshape(OWN, B, width),
        weight,
        block_vals[:, 0],
        out_grad.reshape(-1, B, width),
        own_rows * Z * YC * X,
    )
    return (activations.reshape(own_rows, width), input_grad.reshape(own_rows, width), weight_grad)


def solution(mesh):
    placed = (
        P(("rows", "rep"), None),
        P(),
        P("rows", "rep", None),
        P("rows", "rep", None, None, None),
        P("rows", None),
    )
    return jax.shard_map(
        on_device,
        mesh=mesh,
        in_specs=placed,
        out_specs=(P(("rows", "rep"), None), P(("rows", "rep"), None), P()),
        check_vma=False,
    )
```

```python
import functools
import math

import jax
import jax.numpy as jnp
from jax import lax
from jax.experimental import pallas as pl
from jax.experimental.pallas import tpu as pltpu
from jax.sharding import PartitionSpec as P

MESH = pl.DeviceIdType.MESH
Z = 8
YC = 8
X = 4
B = 128
LANES = 128
OWN = 8
PLANE = X * YC
F32 = jnp.float32
BF16 = jnp.bfloat16


def place():
    r, c = lax.axis_index("rows"), lax.axis_index("rep")
    return r, r // YC, r % YC, c


def greet(device):
    pl.semaphore_signal(pltpu.get_barrier_semaphore(), inc=1, device_id=device, device_id_type=MESH)


def remote(src, dst, send, recv, device):
    return pltpu.make_async_remote_copy(
        src_ref=src, dst_ref=dst, send_sem=send, recv_sem=recv, device_id=device, device_id_type=MESH
    )


def wait_bytes(ref, sem):
    pltpu.make_async_copy(ref, ref, sem).wait()


def layer_kernel(
    scale, own_tab, idx, f_hbm, w_ref, vals_hbm, grad_hbm, act_hbm, ig_hbm, wg_ref, *scratch
):
    ag = [scratch[n * Z : (n + 1) * Z] for n in range(4)]
    at = 4 * Z
    sbuf, src, xs, xr, own = (scratch[at + 4 * i : at + 4 * i + 4] for i in range(5))
    at += 20
    (got, tab, f_ref, act_ref, ig_ref, vals, grad, ft, high, fx, part, r1, a2, r3, r4) = scratch[at : at + 15]
    at += 15
    (t_send, t_recv, l_sem, z_send, z_recv, y_send, y_recv, x_send, x_recv) = scratch[at : at + 9]
    s1, v1, s2, v2, s3, v3, f_send, f_recv = scratch[at + 9 :]
    r, z, yc, c = place()
    half = OWN // 2
    rank = c * YC + yc
    small = part.shape[1] // PLANE
    peers_y = [(z * YC + (yc + 1 + j) % YC, c) for j in range(YC - 1)]
    peers_z = [((z + 1 + i) % Z * YC + yc, c) for i in range(Z - 1)]
    up, down = peers_z[0], peers_z[Z - 2]

    load_features = pltpu.make_async_copy(f_hbm, f_ref, l_sem.at[2])
    load_features.start()

    def in_plane(j):
        t = (rank + j) % PLANE
        return (z * YC + t % YC, t // YC), t

    def greet_plane(j, _):
        greet(in_plane(j)[0])
        return 0

    for device in peers_z:
        greet(device)
    lax.fori_loop(1, PLANE, greet_plane, 0)
    load_grad = pltpu.make_async_copy(grad_hbm.at[pl.ds(c * OWN, OWN)], grad, l_sem.at[1])
    load_vals = [
        pltpu.make_async_copy(vals_hbm.at[:, s], vals.at[:, :, pl.ds(s * B, B)], l_sem.at[3 * s]) for s in range(2)
    ]
    save_act = pltpu.make_async_copy(act_ref, act_hbm, l_sem.at[4])
    save_ig = pltpu.make_async_copy(ig_ref, ig_hbm, l_sem.at[5])

    def columns(h):
        return pl.ds(h * LANES, LANES)

    def mix(h):
        mixed = jnp.dot(f_ref[...].reshape(-1, f_ref.shape[2]), w_ref[:, columns(h)], preferred_element_type=F32)
        ag[h][0][...] = mixed.astype(BF16).reshape(OWN, B, LANES)

    load_features.wait()
    mix(0)
    pl.semaphore_wait(pltpu.get_barrier_semaphore(), PLANE + Z - 2)

    def hop(n, k, forward):
        nxt = (k + 1) % Z if forward else (k - 1) % Z
        source, target = ag[n][k], ag[n][nxt]
        lane = 0 if forward else 1
        if nxt == Z // 2:
            rows = pl.ds(0, half) if forward else pl.ds(half, half)
            source, target = source.at[rows], target.at[rows]
        return remote(source, target, z_send.at[n, nxt, lane], z_recv.at[n, nxt, lane], up if forward else down)

    def arrived(n, k, lane):
        if k == Z // 2:
            chunk = ag[n][k].at[pl.ds(0 if lane == 0 else half, half)]
        else:
            chunk = ag[n][k]
        wait_bytes(chunk, z_recv.at[n, k, lane])

    def serve(n, k):
        column = (z - k + Z) % Z * YC + yc

        def pick(j, _):
            sbuf[n][j * Z + k] = ag[n][k][tab[YC - 2 - j, column]]
            return 0

        lax.fori_loop(0, YC - 1, pick, 0)
        if k == 0:
            for p in range(OWN):
                src[n][YC * Z + p] = ag[n][0][p]
        else:
            src[n][(YC - 1) * Z + k] = ag[n][k][tab[YC - 1, column]]

        def post(j, _):
            slot = j * Z + k
            target = (z * YC + (yc + 1 + j) % YC, c)
            remote(sbuf[n].at[slot], src[n].at[slot], y_send.at[n], y_recv.at[n], target).start()
            return 0

        lax.fori_loop(0, YC - 1, post, 0)

    def products(n, classes):
        for d in classes:
            first = (c + d) % X * OWN

            def pair(q, _):
                totals = []
                for p in (2 * q, 2 * q + 1):
                    b = first + p
                    used = jnp.concatenate([src[n][idx[2 * b]], src[n][idx[2 * b + 1]]], axis=0)
                    totals.append(jnp.dot(vals[b], used, preferred_element_type=F32))
                if d == 0:
                    own[n][2 * q], own[n][2 * q + 1] = totals
                else:
                    at = (d - 1) * OWN + 2 * q
                    xs[n][at], xs[n][at + 1] = [total.astype(BF16) for total in totals]
                    both = pl.ds(at, 2)
                    target = (r, (c + d) % X)
                    remote(xs[n].at[both], xr[n].at[both], x_send.at[n], x_recv.at[n], target).start()
                return 0

            lax.fori_loop(0, OWN // 2, pair, 0)

    def gathered(n):
        wait_bytes(src[n].at[pl.ds(0, (YC - 1) * Z)], y_recv.at[n])

    def summed(n, p):
        a, b, e = (xr[n][d * OWN + p].astype(F32) for d in range(X - 1))
        return (own[n][p] + a) + (b + e)

    def activate(h):
        wait_bytes(xr[h], x_recv.at[h])

        def row(p, _):
            value, slope = silu_parts(summed(h, p))
            act_ref[p, :, columns(h)] = value.astype(BF16)
            ag[2 + h][0][p] = (grad[p, :, columns(h)].astype(F32) * slope).astype(BF16)
            return 0

        lax.fori_loop(0, OWN, row, 0)

    def back(h):
        n = 2 + h
        wait_bytes(xr[n], x_recv.at[n])

        def row(p, _):
            nodes = pl.ds(pl.multiple_of(p * B, B), B)
            high[nodes, columns(h)] = summed(n, p).astype(BF16)
            return 0

        lax.fori_loop(0, OWN, row, 0)

    def flip(d):
        source = f_ref if d == 0 else fx.at[d - 1]
        for p in range(OWN):
            ft[d, :, p * B : (p + 1) * B] = source[p].T

    def terms(h):
        n = 2 + h
        total = jnp.dot(ft[0], own[n][...].astype(BF16).reshape(-1, LANES), preferred_element_type=F32)
        for d in range(1, X):
            sums = xs[n][(d - 1) * OWN : d * OWN].reshape(-1, LANES)
            total += jnp.dot(ft[d], sums, preferred_element_type=F32)
        part[h] = total

    def share_of(h, t):
        return part.at[h, pl.ds(pl.multiple_of(t * small, small), small)]

    def spread(h):
        def post(j, _):
            target, t = in_plane(j)
            remote(share_of(h, t), r1.at[h, j - 1], s1.at[h], v1.at[h], target).start()
            return 0

        lax.fori_loop(1, PLANE, post, 0)

    def collect(h):
        wait_bytes(r1.at[h], v1.at[h])
        total = share_of(h, rank)[...]
        for j in range(PLANE - 1):
            total = total + r1[h, j]
        a2[h] = total
        r3[h, z] = total
        for i in range(Z - 1):
            remote(a2.at[h], r3.at[h, z], s2.at[h, i], v2.at[h, i], peers_z[i]).start()

    def share(h):
        for i in range(Z - 1):
            remote(a2.at[h], r3.at[h, (z + Z - 1 - i) % Z], s2.at[h, i], v2.at[h, i], peers_z[i]).wait()
        total = r3[h, 0]
        for i in range(1, Z):
            total = total + r3[h, i]
        r4[h, rank] = total * scale

        def post(j, _):
            remote(r4.at[h, rank], r4.at[h, rank], s3.at[h], v3.at[h], in_plane(j)[0]).start()
            return 0

        lax.fori_loop(1, PLANE, post, 0)

    def finish(h):
        wait_bytes(r4.at[h, pl.ds(0, PLANE - 1)], v3.at[h])
        wg_ref[:, columns(h)] = r4[h].reshape(-1, LANES)

    def ring(n, step):
        if step < Z // 2:
            arrived(n, step, 0)
            hop(n, step, True).start()
            arrived(n, Z - step, 1)
            hop(n, Z - step, False).start()
            serve(n, step)
            serve(n, Z - step)
        else:
            arrived(n, step, 0)
            arrived(n, step, 1)
            serve(n, step)

    def begin(n):
        hop(n, 0, True).start()
        hop(n, 0, False).start()

    begin(0)
    tables = [remote(own_tab, got.at[j], t_send.at[j], t_recv.at[j], peers_y[j]) for j in range(YC - 1)]
    for copy in tables:
        copy.start()
    fetch = [
        remote(f_ref, fx.at[d - 1], f_send.at[d - 1], f_recv.at[d - 1], (r, (c + X - d) % X)) for d in range(1, X)
    ]
    for copy in fetch:
        copy.start()
    load_grad.start()
    for load in load_vals:
        load.start()
    mix(1)
    for copy in tables:
        copy.wait()
    rows = [got.at[j, 0] for j in range(YC - 1)] + [own_tab.at[0]]
    moves = [pltpu.make_async_copy(row, tab.at[j], l_sem.at[6 + j]) for j, row in enumerate(rows)]
    for move in moves:
        move.start()
    for move in moves:
        move.wait()

    serve(0, 0)
    serve(1, 0)
    flip(0)
    ring(0, 1)
    ring(0, 2)
    ring(0, 3)
    begin(1)
    ring(0, 4)
    load_grad.wait()
    for load in load_vals:
        load.wait()
    ring(1, 1)
    gathered(0)
    products(0, (2, 1))
    ring(1, 2)
    products(0, (3, 0))
    ring(1, 3)
    activate(0)
    begin(2)
    ring(1, 4)
    serve(2, 0)
    for copy in fetch:
        copy.wait()
    flip(1)
    gathered(1)
    products(1, (2, 1))
    ring(2, 1)
    products(1, (3, 0))
    ring(2, 2)
    activate(1)
    save_act.start()
    serve(3, 0)
    ring(2, 3)
    begin(3)
    flip(2)
    ring(2, 4)
    flip(3)
    ring(3, 1)
    gathered(2)
    products(2, (2, 1))
    ring(3, 2)
    products(2, (3, 0))
    ring(3, 3)
    ring(3, 4)
    terms(0)
    spread(0)
    back(0)
    gathered(3)
    products(3, (2, 1, 3, 0))
    terms(1)
    spread(1)
    collect(0)
    collect(1)
    share(0)
    share(1)
    back(1)
    grads = lax.dot_general(high[...], w_ref[...], (((1,), (1,)), ((), ())), preferred_element_type=F32)
    ig_ref[...] = grads.astype(BF16).reshape(ig_ref.shape)
    save_ig.start()
    finish(0)
    finish(1)

    save_act.wait()
    save_ig.wait()
    for h in range(2):
        wait_bytes(r1.at[h], s1.at[h])
        wait_bytes(r4.at[h, pl.ds(0, PLANE - 1)], s3.at[h])
    for n in range(4):
        for k in range(Z // 2):
            hop(n, k, True).wait_send()
            hop(n, (Z - k) % Z, False).wait_send()
        wait_bytes(sbuf[n], y_send.at[n])
        wait_bytes(xs[n], x_send.at[n])


def layer(own_tab, idx, features, weight, vals, out_grad, node_total):
    width = weight.shape[0]
    small = width // PLANE
    blocks = lambda n, kind: pltpu.VMEM((n, B, LANES), kind)
    smem = pl.BlockSpec(memory_space=pltpu.SMEM)
    vmem = pl.BlockSpec(memory_space=pltpu.VMEM)
    hbm = pl.BlockSpec(memory_space=pl.ANY)
    dma = lambda *shape: pltpu.SemaphoreType.DMA(shape)
    wide = jax.ShapeDtypeStruct(features.shape, BF16)
    return pl.pallas_call(
        functools.partial(layer_kernel, 1.0 / math.sqrt(node_total)),
        out_shape=(wide, wide, jax.ShapeDtypeStruct((width, width), F32)),
        in_specs=[vmem, smem, hbm, vmem, hbm, hbm],
        out_specs=(hbm, hbm, vmem),
        scratch_shapes=[blocks(OWN, BF16) for _ in range(4 * Z)]
        + [blocks((YC - 1) * Z, BF16)] * 4
        + [blocks(YC * Z + OWN, BF16)] * 4
        + [blocks((X - 1) * OWN, BF16)] * 8
        + [blocks(OWN, F32)] * 4
        + [
            pltpu.VMEM((YC - 1, 8, LANES), jnp.int32),
            pltpu.SMEM((YC, LANES), jnp.int32),
            pltpu.VMEM(features.shape, BF16),
            pltpu.VMEM(features.shape, BF16),
            pltpu.VMEM(features.shape, BF16),
            pltpu.VMEM((vals.shape[0], B, 2 * B), BF16),
            pltpu.VMEM(features.shape, BF16),
            pltpu.VMEM((X, width, OWN * B), BF16),
            pltpu.VMEM((OWN * B, width), BF16),
            pltpu.VMEM((X - 1, *features.shape), BF16),
            pltpu.VMEM((2, width, LANES), F32),
            pltpu.VMEM((2, PLANE - 1, small, LANES), F32),
            pltpu.VMEM((2, small, LANES), F32),
            pltpu.VMEM((2, Z, small, LANES), F32),
            pltpu.VMEM((2, PLANE, small, LANES), F32),
        ]
        + [dma(YC - 1), dma(YC - 1), dma(6 + YC), dma(4, Z, 2), dma(4, Z, 2), dma(4), dma(4), dma(4), dma(4)]
        + [dma(2)] * 2
        + [dma(2, Z - 1)] * 2
        + [dma(2)] * 2
        + [dma(X - 1)] * 2,
        compiler_params=pltpu.CompilerParams(
            collective_id=0, has_side_effects=True, vmem_limit_bytes=60 * 1024 * 1024
        ),
    )(own_tab, idx, features, weight, vals, out_grad)


def silu_parts(summed):
    sigmoid_vals = jax.nn.sigmoid(summed)
    return (summed * sigmoid_vals, sigmoid_vals * (1.0 + summed * (1.0 - sigmoid_vals)))


def on_device(features, weight, block_cols, block_vals, out_grad):
    own_rows, width = features.shape
    r, z, yc, c = place()
    flat = block_cols[:, 0].reshape(-1)
    owners, places = flat // OWN, flat % OWN
    slot = (yc + YC - 1 - owners % YC) % YC * Z + (z + Z - owners // YC) % Z
    idx = jnp.where(owners == r, YC * Z + places, slot)
    groups = jnp.arange(LANES, dtype=jnp.int32)
    wanted = (owners[:, None] == groups[None, :]) & (owners != r)[:, None]
    table = jnp.sum(jnp.where(wanted, places[:, None], 0), axis=0)
    own_tab = jnp.broadcast_to(table[None], (8, LANES))
    activations, input_grad, weight_grad = layer(
        own_tab,
        idx,
        features.reshape(OWN, B, width),
        weight,
        block_vals[:, 0],
        out_grad.reshape(-1, B, width),
        own_rows * Z * YC * X,
    )
    return (activations.reshape(own_rows, width), input_grad.reshape(own_rows, width), weight_grad)


def solution(mesh):
    placed = (
        P(("rows", "rep"), None),
        P(),
        P("rows", "rep", None),
        P("rows", "rep", None, None, None),
        P("rows", None),
    )
    return jax.shard_map(
        on_device,
        mesh=mesh,
        in_specs=placed,
        out_specs=(P(("rows", "rep"), None), P(("rows", "rep"), None), P()),
        check_vma=False,
    )
```

```python
import functools
import math

import jax
import jax.numpy as jnp
from jax import lax
from jax.experimental import pallas as pl
from jax.experimental.pallas import tpu as pltpu
from jax.sharding import PartitionSpec as P

MESH = pl.DeviceIdType.MESH
Z = 8
YC = 8
X = 4
B = 128
LANES = 128
OWN = 8
PLANE = X * YC
F32 = jnp.float32
BF16 = jnp.bfloat16


def place():
    r, c = lax.axis_index("rows"), lax.axis_index("rep")
    return r, r // YC, r % YC, c


def greet(device):
    pl.semaphore_signal(pltpu.get_barrier_semaphore(), inc=1, device_id=device, device_id_type=MESH)


def remote(src, dst, send, recv, device):
    return pltpu.make_async_remote_copy(
        src_ref=src, dst_ref=dst, send_sem=send, recv_sem=recv, device_id=device, device_id_type=MESH
    )


def wait_bytes(ref, sem):
    pltpu.make_async_copy(ref, ref, sem).wait()


def layer_kernel(
    scale, own_tab, idx, f_hbm, w_ref, vals_hbm, grad_hbm, act_hbm, ig_hbm, wg_ref, *scratch
):
    ag = [scratch[n * Z : (n + 1) * Z] for n in range(4)]
    at = 4 * Z
    sbuf, src, xs, xr, own = (scratch[at + 4 * i : at + 4 * i + 4] for i in range(5))
    at += 20
    (got, tab, f_ref, act_ref, ig_ref, vals, grad, ft, high, fx, part, r1, a2, r3, r4) = scratch[at : at + 15]
    at += 15
    (t_send, t_recv, l_sem, z_send, z_recv, y_send, y_recv, x_send, x_recv) = scratch[at : at + 9]
    s1, v1, s2, v2, s3, v3, f_send, f_recv = scratch[at + 9 :]
    r, z, yc, c = place()
    half = OWN // 2
    rank = c * YC + yc
    small = part.shape[1] // PLANE
    peers_y = [(z * YC + (yc + 1 + j) % YC, c) for j in range(YC - 1)]
    peers_z = [((z + 1 + i) % Z * YC + yc, c) for i in range(Z - 1)]
    up, down = peers_z[0], peers_z[Z - 2]

    load_features = pltpu.make_async_copy(f_hbm, f_ref, l_sem.at[2])
    load_features.start()

    def in_plane(j):
        t = (rank + j) % PLANE
        return (z * YC + t % YC, t // YC), t

    def greet_plane(j, _):
        greet(in_plane(j)[0])
        return 0

    for device in peers_z:
        greet(device)
    lax.fori_loop(1, PLANE, greet_plane, 0)
    load_grad = pltpu.make_async_copy(grad_hbm.at[pl.ds(c * OWN, OWN)], grad, l_sem.at[1])
    load_vals = [
        pltpu.make_async_copy(vals_hbm.at[:, s], vals.at[:, :, pl.ds(s * B, B)], l_sem.at[3 * s]) for s in range(2)
    ]
    save_act = pltpu.make_async_copy(act_ref, act_hbm, l_sem.at[4])
    save_ig = pltpu.make_async_copy(ig_ref, ig_hbm, l_sem.at[5])

    def columns(h):
        return pl.ds(h * LANES, LANES)

    def mix(h):
        mixed = jnp.dot(f_ref[...].reshape(-1, f_ref.shape[2]), w_ref[:, columns(h)], preferred_element_type=F32)
        ag[h][0][...] = mixed.astype(BF16).reshape(OWN, B, LANES)

    load_features.wait()
    mix(0)
    pl.semaphore_wait(pltpu.get_barrier_semaphore(), PLANE + Z - 2)

    def hop(n, k, forward):
        nxt = (k + 1) % Z if forward else (k - 1) % Z
        source, target = ag[n][k], ag[n][nxt]
        lane = 0 if forward else 1
        if nxt == Z // 2:
            rows = pl.ds(0, half) if forward else pl.ds(half, half)
            source, target = source.at[rows], target.at[rows]
        return remote(source, target, z_send.at[n, nxt, lane], z_recv.at[n, nxt, lane], up if forward else down)

    def arrived(n, k, lane):
        if k == Z // 2:
            chunk = ag[n][k].at[pl.ds(0 if lane == 0 else half, half)]
        else:
            chunk = ag[n][k]
        wait_bytes(chunk, z_recv.at[n, k, lane])

    def serve(n, k):
        column = (z - k + Z) % Z * YC + yc

        def pick(j, _):
            sbuf[n][j * Z + k] = ag[n][k][tab[YC - 2 - j, column]]
            return 0

        lax.fori_loop(0, YC - 1, pick, 0)
        if k == 0:
            for p in range(OWN):
                src[n][YC * Z + p] = ag[n][0][p]
        else:
            src[n][(YC - 1) * Z + k] = ag[n][k][tab[YC - 1, column]]

        def post(j, _):
            slot = j * Z + k
            target = (z * YC + (yc + 1 + j) % YC, c)
            remote(sbuf[n].at[slot], src[n].at[slot], y_send.at[n], y_recv.at[n], target).start()
            return 0

        lax.fori_loop(0, YC - 1, post, 0)

    def products(n, classes):
        for d in classes:
            first = (c + d) % X * OWN

            def pair(q, _):
                totals = []
                for p in (2 * q, 2 * q + 1):
                    b = first + p
                    used = jnp.concatenate([src[n][idx[2 * b]], src[n][idx[2 * b + 1]]], axis=0)
                    totals.append(jnp.dot(vals[b], used, preferred_element_type=F32))
                if d == 0:
                    own[n][2 * q], own[n][2 * q + 1] = totals
                else:
                    at = (d - 1) * OWN + 2 * q
                    xs[n][at], xs[n][at + 1] = [total.astype(BF16) for total in totals]
                    both = pl.ds(at, 2)
                    target = (r, (c + d) % X)
                    remote(xs[n].at[both], xr[n].at[both], x_send.at[n], x_recv.at[n], target).start()
                return 0

            lax.fori_loop(0, OWN // 2, pair, 0)

    def gathered(n):
        wait_bytes(src[n].at[pl.ds(0, (YC - 1) * Z)], y_recv.at[n])

    def summed(n, p):
        a, b, e = (xr[n][d * OWN + p].astype(F32) for d in range(X - 1))
        return (own[n][p] + a) + (b + e)

    def activate(h):
        wait_bytes(xr[h], x_recv.at[h])

        def row(p, _):
            value, slope = silu_parts(summed(h, p))
            act_ref[p, :, columns(h)] = value.astype(BF16)
            ag[2 + h][0][p] = (grad[p, :, columns(h)].astype(F32) * slope).astype(BF16)
            return 0

        lax.fori_loop(0, OWN, row, 0)

    def back(h):
        n = 2 + h
        wait_bytes(xr[n], x_recv.at[n])

        def row(p, _):
            nodes = pl.ds(pl.multiple_of(p * B, B), B)
            high[nodes, columns(h)] = summed(n, p).astype(BF16)
            return 0

        lax.fori_loop(0, OWN, row, 0)

    def flip(d):
        source = f_ref if d == 0 else fx.at[d - 1]
        for p in range(OWN):
            ft[d, :, p * B : (p + 1) * B] = source[p].T

    def terms(h):
        n = 2 + h
        total = jnp.dot(ft[0], own[n][...].astype(BF16).reshape(-1, LANES), preferred_element_type=F32)
        for d in range(1, X):
            sums = xs[n][(d - 1) * OWN : d * OWN].reshape(-1, LANES)
            total += jnp.dot(ft[d], sums, preferred_element_type=F32)
        part[h] = total

    def share_of(h, t):
        return part.at[h, pl.ds(pl.multiple_of(t * small, small), small)]

    def spread(h):
        def post(j, _):
            target, t = in_plane(j)
            remote(share_of(h, t), r1.at[h, j - 1], s1.at[h], v1.at[h], target).start()
            return 0

        lax.fori_loop(1, PLANE, post, 0)

    def collect(h):
        wait_bytes(r1.at[h], v1.at[h])
        total = share_of(h, rank)[...]
        for j in range(PLANE - 1):
            total = total + r1[h, j]
        a2[h] = total
        r3[h, z] = total
        for i in range(Z - 1):
            remote(a2.at[h], r3.at[h, z], s2.at[h, i], v2.at[h, i], peers_z[i]).start()

    def share(h):
        for i in range(Z - 1):
            remote(a2.at[h], r3.at[h, (z + Z - 1 - i) % Z], s2.at[h, i], v2.at[h, i], peers_z[i]).wait()
        total = r3[h, 0]
        for i in range(1, Z):
            total = total + r3[h, i]
        r4[h, rank] = total * scale

        def post(j, _):
            remote(r4.at[h, rank], r4.at[h, rank], s3.at[h], v3.at[h], in_plane(j)[0]).start()
            return 0

        lax.fori_loop(1, PLANE, post, 0)

    def finish(h):
        wait_bytes(r4.at[h, pl.ds(0, PLANE - 1)], v3.at[h])
        wg_ref[:, columns(h)] = r4[h].reshape(-1, LANES)

    def ring(n, step):
        if step < Z // 2:
            arrived(n, step, 0)
            hop(n, step, True).start()
            arrived(n, Z - step, 1)
            hop(n, Z - step, False).start()
            serve(n, step)
            serve(n, Z - step)
        else:
            arrived(n, step, 0)
            arrived(n, step, 1)
            serve(n, step)

    def begin(n):
        hop(n, 0, True).start()
        hop(n, 0, False).start()

    begin(0)
    tables = [remote(own_tab, got.at[j], t_send.at[j], t_recv.at[j], peers_y[j]) for j in range(YC - 1)]
    for copy in tables:
        copy.start()
    fetch = [
        remote(f_ref, fx.at[d - 1], f_send.at[d - 1], f_recv.at[d - 1], (r, (c + X - d) % X)) for d in range(1, X)
    ]
    for copy in fetch:
        copy.start()
    load_grad.start()
    for load in load_vals:
        load.start()
    mix(1)
    for copy in tables:
        copy.wait()
    rows = [got.at[j, 0] for j in range(YC - 1)] + [own_tab.at[0]]
    moves = [pltpu.make_async_copy(row, tab.at[j], l_sem.at[6 + j]) for j, row in enumerate(rows)]
    for move in moves:
        move.start()
    for move in moves:
        move.wait()

    serve(0, 0)
    serve(1, 0)
    flip(0)
    ring(0, 1)
    ring(0, 2)
    ring(0, 3)
    begin(1)
    ring(0, 4)
    load_grad.wait()
    for load in load_vals:
        load.wait()
    ring(1, 1)
    gathered(0)
    products(0, (2, 1))
    ring(1, 2)
    products(0, (3, 0))
    ring(1, 3)
    activate(0)
    begin(2)
    ring(1, 4)
    serve(2, 0)
    for copy in fetch:
        copy.wait()
    flip(1)
    gathered(1)
    products(1, (2, 1))
    ring(2, 1)
    products(1, (3, 0))
    ring(2, 2)
    activate(1)
    save_act.start()
    serve(3, 0)
    ring(2, 3)
    begin(3)
    flip(2)
    ring(2, 4)
    flip(3)
    ring(3, 1)
    gathered(2)
    products(2, (2, 1))
    ring(3, 2)
    products(2, (3, 0))
    ring(3, 3)
    ring(3, 4)
    terms(0)
    spread(0)
    back(0)
    collect(0)
    gathered(3)
    products(3, (2, 1, 3, 0))
    terms(1)
    spread(1)
    share(0)
    collect(1)
    share(1)
    back(1)
    grads = lax.dot_general(high[...], w_ref[...], (((1,), (1,)), ((), ())), preferred_element_type=F32)
    ig_ref[...] = grads.astype(BF16).reshape(ig_ref.shape)
    save_ig.start()
    finish(0)
    finish(1)

    save_act.wait()
    save_ig.wait()
    for h in range(2):
        wait_bytes(r1.at[h], s1.at[h])
        wait_bytes(r4.at[h, pl.ds(0, PLANE - 1)], s3.at[h])
    for n in range(4):
        for k in range(Z // 2):
            hop(n, k, True).wait_send()
            hop(n, (Z - k) % Z, False).wait_send()
        wait_bytes(sbuf[n], y_send.at[n])
        wait_bytes(xs[n], x_send.at[n])


def layer(own_tab, idx, features, weight, vals, out_grad, node_total):
    width = weight.shape[0]
    small = width // PLANE
    blocks = lambda n, kind: pltpu.VMEM((n, B, LANES), kind)
    smem = pl.BlockSpec(memory_space=pltpu.SMEM)
    vmem = pl.BlockSpec(memory_space=pltpu.VMEM)
    hbm = pl.BlockSpec(memory_space=pl.ANY)
    dma = lambda *shape: pltpu.SemaphoreType.DMA(shape)
    wide = jax.ShapeDtypeStruct(features.shape, BF16)
    return pl.pallas_call(
        functools.partial(layer_kernel, 1.0 / math.sqrt(node_total)),
        out_shape=(wide, wide, jax.ShapeDtypeStruct((width, width), F32)),
        in_specs=[vmem, smem, hbm, vmem, hbm, hbm],
        out_specs=(hbm, hbm, vmem),
        scratch_shapes=[blocks(OWN, BF16) for _ in range(4 * Z)]
        + [blocks((YC - 1) * Z, BF16)] * 4
        + [blocks(YC * Z + OWN, BF16)] * 4
        + [blocks((X - 1) * OWN, BF16)] * 8
        + [blocks(OWN, F32)] * 4
        + [
            pltpu.VMEM((YC - 1, 8, LANES), jnp.int32),
            pltpu.SMEM((YC, LANES), jnp.int32),
            pltpu.VMEM(features.shape, BF16),
            pltpu.VMEM(features.shape, BF16),
            pltpu.VMEM(features.shape, BF16),
            pltpu.VMEM((vals.shape[0], B, 2 * B), BF16),
            pltpu.VMEM(features.shape, BF16),
            pltpu.VMEM((X, width, OWN * B), BF16),
            pltpu.VMEM((OWN * B, width), BF16),
            pltpu.VMEM((X - 1, *features.shape), BF16),
            pltpu.VMEM((2, width, LANES), F32),
            pltpu.VMEM((2, PLANE - 1, small, LANES), F32),
            pltpu.VMEM((2, small, LANES), F32),
            pltpu.VMEM((2, Z, small, LANES), F32),
            pltpu.VMEM((2, PLANE, small, LANES), F32),
        ]
        + [dma(YC - 1), dma(YC - 1), dma(6 + YC), dma(4, Z, 2), dma(4, Z, 2), dma(4), dma(4), dma(4), dma(4)]
        + [dma(2)] * 2
        + [dma(2, Z - 1)] * 2
        + [dma(2)] * 2
        + [dma(X - 1)] * 2,
        compiler_params=pltpu.CompilerParams(
            collective_id=0, has_side_effects=True, vmem_limit_bytes=60 * 1024 * 1024
        ),
    )(own_tab, idx, features, weight, vals, out_grad)


def silu_parts(summed):
    sigmoid_vals = jax.nn.sigmoid(summed)
    return (summed * sigmoid_vals, sigmoid_vals * (1.0 + summed * (1.0 - sigmoid_vals)))


def on_device(features, weight, block_cols, block_vals, out_grad):
    own_rows, width = features.shape
    r, z, yc, c = place()
    flat = block_cols[:, 0].reshape(-1)
    owners, places = flat // OWN, flat % OWN
    slot = (yc + YC - 1 - owners % YC) % YC * Z + (z + Z - owners // YC) % Z
    idx = jnp.where(owners == r, YC * Z + places, slot)
    groups = jnp.arange(LANES, dtype=jnp.int32)
    wanted = (owners[:, None] == groups[None, :]) & (owners != r)[:, None]
    table = jnp.sum(jnp.where(wanted, places[:, None], 0), axis=0)
    own_tab = jnp.broadcast_to(table[None], (8, LANES))
    activations, input_grad, weight_grad = layer(
        own_tab,
        idx,
        features.reshape(OWN, B, width),
        weight,
        block_vals[:, 0],
        out_grad.reshape(-1, B, width),
        own_rows * Z * YC * X,
    )
    return (activations.reshape(own_rows, width), input_grad.reshape(own_rows, width), weight_grad)


def solution(mesh):
    placed = (
        P(("rows", "rep"), None),
        P(),
        P("rows", "rep", None),
        P("rows", "rep", None, None, None),
        P("rows", None),
    )
    return jax.shard_map(
        on_device,
        mesh=mesh,
        in_specs=placed,
        out_specs=(P(("rows", "rep"), None), P(("rows", "rep"), None), P()),
        check_vma=False,
    )
```
